512 devices in a mesh: gx: 16 (over y, z_lo), gy: 8 (over x, core), gz: 4 (over z_hi).
Axes of the slice: x: 4, y: 4, z: 16 (z_hi: 4, z_lo: 4; z = z_hi * 4 + z_lo), core: 2. Of those that a mesh axis runs over, the one named last changes fastest.
Arguments:
- positions: float32 [16, 8, 4, 3, 64], P('gx', 'gy', 'gz'), may hold values from 0 to 5
- species: int32 [16, 8, 4, 64], P('gx', 'gy', 'gz'), may hold values from 0 to 7
- counts: int32 [16, 8, 4], P('gx', 'gy', 'gz'), may hold values from 4 to 64, as said below
- embed: bfloat16 [8, 128], replicated, may hold values from -6 to 6
- radial_one: float32 [2, 4, 128], replicated, may hold values from -6 to 6
- mix_one: bfloat16 [128, 256], replicated, may hold values from -0.375 to 0.375
- read_one: float32 [128], replicated, may hold values from -0.5 to 0.5
- radial_two: float32 [4, 128], replicated, may hold values from -6 to 6
- mix_two: bfloat16 [128, 128], replicated, may hold values from -0.5 to 0.5
- read_hidden: bfloat16 [16, 128], replicated, may hold values from -0.5 to 0.5
- read_out: float32 [16], replicated, may hold values from -1.5 to 1.5
Outputs:
- forces: float32 [16, 8, 4, 3, 64], P('gx', 'gy', 'gz')
- energies: float32 [16, 8, 4, 64], P('gx', 'gy', 'gz')
- features: bfloat16 [16, 8, 4, 128, 64], P('gx', 'gy', 'gz')
The draws below stay inside these ranges and needn't reach their ends.
Inputs may be any that keep to these rules, and one draw needn't show every extreme that they name: `counts`: the first block of the grid holds exactly 64 live atoms.
All inputs are finite; a program needn't handle non-finite values.
Results may differ from the reference program's by a relative error of at most 0.018.
Values may be sent and summed in bfloat16 or wider, within the bound.
A program may use at most 64 MiB of HBM per device.

```python
import functools
import math
import jax
import jax.numpy as jnp
from jax import lax

C = 128
ATOMS = 64
NB = 4
NSPEC = 8
READ = 16
NX = 16
NY = 8
NZ = 4


def draw_counts(key, part):
    values = jax.random.randint(key, (NX, NY, NZ), max(1, ATOMS // 16), ATOMS + 1)
    return values.at[0, 0, 0].set(ATOMS).astype(jnp.int32)


def with_ends(values, stream_key, low, high):
    longest = values.shape.index(max(values.shape))
    spots = []
    for shift in (0, 1):
        where = [jax.random.randint(jax.random.fold_in(stream_key, axis), (), 0, length) for axis, length in enumerate(values.shape)]
        where[longest] = (where[longest] + shift) % values.shape[longest]
        spots.append(tuple(where))
    return values.at[spots[0]].set(low).at[spots[1]].set(high)


def block_levels(stream_key, shape, shards, low, largest):
    gain = 1.0
    for position, shards_of in shards:
        heights = jax.random.uniform(jax.random.fold_in(jax.random.fold_in(stream_key, 6), position), (shards_of,), jnp.float32, low / len(shards), largest / len(shards))
        gain = gain * jnp.repeat(jnp.exp(heights), shape[position] // shards_of).reshape((-1,) + (1,) * (len(shape) - 1 - position))
    return gain


def normal_values(key, shape, deviation, limit, kind=jnp.bfloat16):
    values = jax.random.normal(key, shape, jnp.float32) * deviation
    return jnp.minimum(jnp.maximum(values, -limit), limit).astype(kind)


def setup_inputs(seed: int = 0) -> dict:
    keys = jax.random.split(jax.random.key(seed), 12)
    positions = jnp.clip(5.0 * jax.random.uniform(keys[0], (NX, NY, NZ, 3, ATOMS), jnp.float32) ** block_levels(keys[0], (NX, NY, NZ, 3, ATOMS), ((0, 16), (1, 8), (2, 4)), -0.2, 0.2), 0.0, 5.0)
    species = with_ends(jax.random.randint(keys[1], (NX, NY, NZ, ATOMS), 0, NSPEC), jax.random.fold_in(keys[1], 1), 0, NSPEC - 1).astype(jnp.int32)
    counts = draw_counts(jax.random.fold_in(keys[11], 71), 0)
    embed = normal_values(keys[3], (NSPEC, C), 1.0, 6.0)
    radial_one = normal_values(keys[4], (2, NB, C), 1.0, 6.0, jnp.float32)
    mix_one = normal_values(keys[5], (C, 2 * C), (2 * C) ** -0.5, 0.375)
    read_one = normal_values(keys[6], (C,), C ** -0.5, 0.5, jnp.float32)
    radial_two = normal_values(keys[7], (NB, C), 1.0, 6.0, jnp.float32)
    mix_two = normal_values(keys[8], (C, C), C ** -0.5, 0.5)
    read_hidden = normal_values(keys[9], (READ, C), C ** -0.5, 0.5)
    read_out = normal_values(keys[10], (READ,), READ ** -0.5, 1.5, jnp.float32)
    return dict(positions=positions, species=species, counts=counts, embed=embed, radial_one=radial_one, mix_one=mix_one, read_one=read_one, radial_two=radial_two, mix_two=mix_two, read_hidden=read_hidden, read_out=read_out)


CELL_SIDE = 5.0
CUT_SQUARE = 25.0
SOFTEN = 0.25
MSG_SCALE = 0.05
ROOT_THREE = math.sqrt(3.0)
OFFSETS = [(first, second, third) for first in (-1, 0, 1) for second in (-1, 0, 1) for third in (-1, 0, 1)]

def pair_terms(own_coords, far_coords, own_live, far_live, offset, nbasis, vectors):
    displace = jnp.array(offset, jnp.float32) * CELL_SIDE
    separation = far_coords[..., :, None, :] + displace[:, None, None] - own_coords[..., :, :, None]
    dist_sq = lax.optimization_barrier(jnp.sum(separation * separation, axis=-3)) + SOFTEN
    inverse = lax.rsqrt(dist_sq)
    radius = dist_sq * inverse
    envelope = jnp.square(jnp.maximum(1.0 - dist_sq / CUT_SQUARE, 0.0))
    pair_mask = own_live[..., :, None] & far_live[..., None, :]
    if offset == (0, 0, 0):
        slot_index = jnp.arange(own_coords.shape[-1])
        pair_mask = pair_mask & (slot_index[:, None] != slot_index[None, :])
    radial = envelope * inverse * pair_mask.astype(jnp.float32)
    waves = (jnp.arange(nbasis) + 1).astype(jnp.float32) * (math.pi / CELL_SIDE)
    basis = jnp.sin(waves[:, None, None] * radius[..., None, :, :]) * radial[..., None, :, :]
    scalar_mat = basis.astype(jnp.bfloat16)
    if not vectors:
        return scalar_mat
    unit = ROOT_THREE * separation * inverse[..., None, :, :]
    vector_mat = (unit[..., :, None, :, :] * basis[..., None, :, :, :]).astype(jnp.bfloat16)
    return (scalar_mat, vector_mat)

def first_term(own_coords, far_coords, own_live, far_live, far_weights, offset):
    nbasis = far_weights.shape[-3]
    scalar_mat, vector_mat = pair_terms(own_coords, far_coords, own_live, far_live, offset, nbasis, True)
    scalar_msg = jnp.einsum('...ncj,...nij->...ci', far_weights[..., 0, :, :, :].astype(jnp.float32), scalar_mat.astype(jnp.float32))
    vector_msg = jnp.einsum('...ncj,...knij->...kci', far_weights[..., 1, :, :, :].astype(jnp.float32), vector_mat.astype(jnp.float32))
    return (scalar_msg, vector_msg)

def second_term(own_coords, far_coords, own_live, far_live, far_weights, offset):
    nbasis = far_weights.shape[-3]
    scalar_mat = pair_terms(own_coords, far_coords, own_live, far_live, offset, nbasis, False)
    return jnp.einsum('...ncj,...nij->...ci', far_weights.astype(jnp.float32), scalar_mat.astype(jnp.float32))

def rolled(array, offset):
    return jnp.roll(array, (-offset[0], -offset[1], -offset[2]), axis=(0, 1, 2))

def reference(positions, species, counts, embed, radial_one, mix_one, read_one, radial_two, mix_two, read_hidden, read_out):
    slot_index = jnp.arange(positions.shape[-1])
    occupied = slot_index < counts[..., None]
    element = jnp.where(occupied, species, -1)
    onehot = (element[..., None, :] == jnp.arange(embed.shape[0])[:, None]).astype(jnp.float32)
    embedded = jnp.einsum('sc,xyzsa->xyzca', embed.astype(jnp.float32), onehot).astype(jnp.bfloat16)
    weighted_one = (radial_one[:, :, :, None] * embedded[..., None, None, :, :].astype(jnp.float32)).astype(jnp.bfloat16)

    def layers(coords):
        scalar_msg = jnp.zeros(embedded.shape, jnp.float32)
        vector_msg = jnp.zeros(embedded.shape[:3] + (3,) + embedded.shape[3:], jnp.float32)
        for offset in OFFSETS:
            term = jax.checkpoint(functools.partial(first_term, offset=offset))
            part_scalar, part_vector = term(coords, rolled(coords, offset), occupied, rolled(occupied, offset), rolled(weighted_one, offset))
            scalar_msg = scalar_msg + part_scalar
            vector_msg = vector_msg + part_vector
        scalar_msg = MSG_SCALE * scalar_msg
        vector_msg = MSG_SCALE * vector_msg
        invariants = jnp.concatenate([scalar_msg, lax.optimization_barrier(jnp.sum(vector_msg * vector_msg, axis=-3))], axis=-2).astype(jnp.bfloat16)
        mixing = jnp.einsum('dc,...ca->...da', mix_one.astype(jnp.float32), invariants.astype(jnp.float32))
        layer_one = (embedded.astype(jnp.float32) + jax.nn.silu(mixing)).astype(jnp.bfloat16)
        weighted_two = (radial_two[:, :, None] * layer_one[..., None, :, :].astype(jnp.float32)).astype(jnp.bfloat16)
        message_two = jnp.zeros(embedded.shape, jnp.float32)
        for offset in OFFSETS:
            term = jax.checkpoint(functools.partial(second_term, offset=offset))
            message_two = message_two + term(coords, rolled(coords, offset), occupied, rolled(occupied, offset), rolled(weighted_two, offset))
        rounded_two = (MSG_SCALE * message_two).astype(jnp.bfloat16)
        mixing_two = jnp.einsum('dc,...ca->...da', mix_two.astype(jnp.float32), rounded_two.astype(jnp.float32))
        features = (layer_one.astype(jnp.float32) + jax.nn.silu(mixing_two)).astype(jnp.bfloat16)
        hidden = jax.nn.silu(jnp.einsum('mc,...ca->...ma', read_hidden.astype(jnp.float32), features.astype(jnp.float32)))
        energy = jnp.einsum('c,...ca->...a', read_one, layer_one.astype(jnp.float32)) + jnp.einsum('m,...ma->...a', read_out, hidden)
        energy = energy * occupied.astype(jnp.float32)
        return (energy, features)
    energy, pullback, features = jax.vjp(layers, positions, has_aux=True)
    gradient, = pullback(jnp.ones_like(energy))
    return (-gradient, energy, features)
```

```python
import functools
import math

import jax
import jax.numpy as jnp
from jax import lax
from jax.experimental import pallas as pl
from jax.experimental.pallas import tpu as pltpu
from jax.sharding import PartitionSpec as P

CELL_SIDE = 5.0
CUT_SQUARE = 25.0
SOFTEN = 0.25
MSG_SCALE = 0.05
ROOT_THREE = math.sqrt(3.0)
WAVE = math.pi / CELL_SIDE
FAR = 1000.0
MESH = pl.DeviceIdType.MESH
OFFSETS = 27
CENTRE = 13
CHUNKS = 14
LANES = 128
PIECE = 16
COMPACT = True
BF16 = jnp.bfloat16
F32 = jnp.float32


def nt(a, b):
    return lax.dot_general(a, b, (((1,), (1,)), ((), ())), preferred_element_type=F32)


def nn(a, b):
    return jnp.dot(a, b, preferred_element_type=F32)


def sigmoid(v):
    return 1.0 / (1.0 + jnp.exp(-v))


def silu_slope(v, s):
    return s * (1.0 + v * (1.0 - s))


def cos_sin(y):
    q = y * y
    c = 1.0 / 479001600.0
    for term in (-1.0 / 3628800.0, 1.0 / 40320.0, -1.0 / 720.0, 1.0 / 24.0, -0.5, 1.0):
        c = c * q + term
    s = -1.0 / 39916800.0
    for term in (1.0 / 362880.0, -1.0 / 5040.0, 1.0 / 120.0, -1.0 / 6.0, 1.0):
        s = s * q + term
    return c, s * y


def block_of(gx, gy, gz, shape):
    nx, _, nz = shape
    if not COMPACT:
        return gx, gy, gz
    run = nx // nz
    return gz * run + lax.rem(gx, run), gy, gx // run


def kernel(
    shape,
    packet,
    embed,
    radial_one,
    mix_one,
    read_one,
    radial_two,
    mix_two,
    read_hidden,
    read_out_col,
    read_out_row,
    out,
    feats,
    slots,
    halo,
    mine,
    ghosts_out,
    ghosts_in,
    own,
    diag,
    vs,
    sm,
    hot,
    pre,
    d1,
    acc,
    pair_lhs,
    send,
    recv,
):
    nx, ny, nz = shape
    here = block_of(lax.axis_index("gx"), lax.axis_index("gy"), lax.axis_index("gz"), shape)

    def offset_of(t):
        return t + jnp.where(t >= CENTRE, 1, 0)

    def parts(o):
        return o // 9 - 1, lax.rem(o // 3, 3) - 1, lax.rem(o, 3) - 1

    def device(o, sign):
        ox, oy, oz = parts(o)
        bx = lax.rem(here[0] + sign * ox + nx, nx)
        by = lax.rem(here[1] + sign * oy + ny, ny)
        bz = lax.rem(here[2] + sign * oz + nz, nz)
        return block_of(bx, by, bz, shape)

    def copy_of(phase, o, sign):
        if phase == 0:
            src, dst = packet, slots.at[o]
        elif phase == 3:
            src, dst = ghosts_out.at[o // 2], ghosts_in.at[o]
        else:
            half = pl.ds((phase - 1) * LANES, LANES)
            src, dst = mine.at[phase - 1], halo.at[pl.ds(o * 64, 64), half]
        return pltpu.make_async_remote_copy(
            src_ref=src,
            dst_ref=dst,
            send_sem=send.at[phase, o],
            recv_sem=recv.at[phase, o],
            device_id=device(o, sign),
            device_id_type=MESH,
        )

    def start_all(phase, sign):
        def step(t, carry):
            copy_of(phase, offset_of(t), sign).start()
            return carry

        lax.fori_loop(0, OFFSETS - 1, step, 0)

    def arrived_all(phase, sign):
        def step(t, carry):
            copy_of(phase, offset_of(t), sign).wait_recv()
            return carry

        lax.fori_loop(0, OFFSETS - 1, step, 0)

    def sent_all(phase, sign):
        def step(t, carry):
            copy_of(phase, offset_of(t), sign).wait_send()
            return carry

        lax.fori_loop(0, OFFSETS - 1, step, 0)

    barrier = pltpu.get_barrier_semaphore()

    def greet(t, carry):
        pl.semaphore_signal(
            barrier, inc=1, device_id=device(offset_of(t), 1), device_id_type=MESH
        )
        return carry

    lax.fori_loop(0, OFFSETS - 1, greet, 0)

    mine_packet = packet[...]
    column = jnp.transpose(mine_packet)[0:64, :]
    live_col = jnp.where(column[:, 3:4] >= 0.0, 1.0, 0.0)
    for k in range(3):
        place = jnp.where(live_col > 0.0, column[:, k : k + 1], -FAR)
        own[k] = jnp.broadcast_to(place, (64, LANES))
    live_row = jnp.where(mine_packet[3:4, 0:64] >= 0.0, 1.0, 0.0)
    row_id = lax.broadcasted_iota(jnp.int32, (64, LANES), 0)
    lane_id = lax.broadcasted_iota(jnp.int32, (64, LANES), 1)
    diag[...] = jnp.where(row_id + 64 == lane_id, CUT_SQUARE, 0.0)
    species_id = lax.broadcasted_iota(jnp.int32, (64, 8), 1).astype(F32)
    own_hot = jnp.where(column[:, 3:4] == species_id, 1.0, 0.0).astype(BF16)
    embed_wide = embed[...].astype(F32)
    own_embed = nn(own_hot, embed[...])
    tables = []
    for g in range(2):
        rows = [radial_one[g, n : n + 1, :] * embed_wide for n in range(4)]
        tables.append(jnp.concatenate(rows, axis=0).astype(BF16))
    table_scalar, table_vector = tables
    slots[CENTRE] = mine_packet
    pad_row = lax.broadcasted_iota(jnp.int32, (8, LANES), 0)
    slots[OFFSETS] = jnp.where(pad_row < 3, FAR, -1.0)
    halo[OFFSETS * 64 :, :] = jnp.zeros((64, 2 * LANES), BF16)
    low = lax.broadcasted_iota(jnp.int32, (1, LANES), 1) < 64
    hot_row = lax.broadcasted_iota(jnp.int32, (32, LANES), 0).astype(F32)

    pl.semaphore_wait(barrier, OFFSETS - 1)
    start_all(0, -1)
    arrived_all(0, -1)

    def far_rows(m):
        first, second = slots[2 * m], slots[2 * m + 1]
        shift_first, shift_second = parts(2 * m), parts(2 * m + 1)
        rows = []
        for k in range(3):
            a = first[k : k + 1, :] + shift_first[k].astype(F32) * CELL_SIDE
            b = second[k : k + 1, :] + shift_second[k].astype(F32) * CELL_SIDE
            rows.append(jnp.where(low, a, b))
        return rows, jnp.where(low, first[3:4, :], second[3:4, :])

    def geometry(places, m, top):
        rows = pl.ds(top, PIECE)
        sep = [places[k] - own[k, rows, :] for k in range(3)]
        dist = sep[0] * sep[0] + sep[1] * sep[1] + sep[2] * sep[2] + SOFTEN
        self_pair = jnp.where(m == CENTRE // 2, 1.0, 0.0)
        dist = jnp.minimum(dist + diag[rows, :] * self_pair, CUT_SQUARE)
        inverse = lax.rsqrt(dist)
        edge = (CUT_SQUARE - dist) * (1.0 / CUT_SQUARE)
        angle = dist * inverse * WAVE - 0.5 * math.pi
        sine, minus_cosine = cos_sin(angle)
        double = -2.0 * minus_cosine
        sines = [sine, double * sine]
        sines.append(double * sines[1] - sines[0])
        sines.append(double * sines[2] - sines[1])
        return sep, inverse, edge, sines, double

    def forward(m, carry):
        places, kinds = far_rows(m)
        for n in range(4):
            hit = jnp.where(kinds == hot_row - 8.0 * n, 1.0, 0.0).astype(BF16)
            hot[:, pl.ds(pl.multiple_of(m * 512 + n * LANES, LANES), LANES)] = hit
        for top in range(0, 64, PIECE):
            sep, inverse, edge, sines, _ = geometry(places, m, top)
            weight = edge * edge * inverse
            scaled = inverse * ROOT_THREE
            units = [s * scaled for s in sep]
            for n in range(4):
                basis = sines[n] * weight
                narrow = basis.astype(BF16)
                wide_cols = pl.ds(pl.multiple_of(m * 512 + n * LANES, LANES), LANES)
                cols = pl.ds(pl.multiple_of(m * LANES, LANES), LANES)
                sm[n * 64 + top : n * 64 + top + PIECE, cols] = narrow
                vs[top : top + PIECE, wide_cols] = narrow
                for k in range(3):
                    at = 64 * (k + 1) + top
                    vs[at : at + PIECE, wide_cols] = (units[k] * basis).astype(BF16)
        return carry

    lax.fori_loop(0, CHUNKS, forward, 0)

    def gather_kinds(j, total):
        cols = pl.ds(pl.multiple_of(j * 1024, 1024), 1024)
        return total + nt(vs[:, cols], hot[:, cols])

    kinds_sum = lax.fori_loop(0, 7, gather_kinds, jnp.zeros((256, 32), F32))
    high = kinds_sum.astype(BF16)
    rest = (kinds_sum - high.astype(F32)).astype(BF16)
    scalar_msg = MSG_SCALE * (nn(high[0:64], table_scalar) + nn(rest[0:64], table_scalar))
    vector_msg = MSG_SCALE * (nn(high[64:], table_vector) + nn(rest[64:], table_vector))
    squares = vector_msg * vector_msg
    norm = squares[0:64] + squares[64:128] + squares[128:192]
    invariants = jnp.concatenate([scalar_msg, norm], axis=1).astype(BF16)
    mixing = nt(invariants, mix_one[...])
    gate = sigmoid(mixing)
    layer_one = (own_embed + mixing * gate).astype(BF16)
    mine[0] = layer_one
    halo[CENTRE * 64 : CENTRE * 64 + 64, 0:LANES] = layer_one
    start_all(1, -1)

    def slopes(m, carry):
        places, _ = far_rows(m)
        cols = pl.ds(pl.multiple_of(m * LANES, LANES), LANES)
        for top in range(0, 64, PIECE):
            sep, inverse, edge, sines, double = geometry(places, m, top)
            weight = edge * edge * inverse
            fall = -edge * (4.0 / CUT_SQUARE + edge * inverse * inverse)
            cosines = [0.5 * double, 0.5 * double * double - 1.0]
            cosines.append(double * cosines[1] - cosines[0])
            cosines.append(double * cosines[2] - cosines[1])
            rows = pl.ds(top, PIECE)
            for k in range(3):
                pre[k, rows, cols] = sep[k]
            pre[3, rows, cols] = inverse
            for n in range(4):
                pre[4 + n, rows, cols] = sines[n] * weight
                turn = cosines[n] * ((n + 1) * WAVE)
                pre[8 + n, rows, cols] = turn * weight + sines[n] * fall
        return carry

    lax.fori_loop(0, CHUNKS, slopes, 0)
    arrived_all(1, -1)

    def spread(half):
        def step(j, total):
            rows = pl.ds(pl.multiple_of(j * 256, 256), 256)
            return total + nn(sm[:, rows], halo[rows, half * LANES : (half + 1) * LANES])

        total = lax.fori_loop(0, 7, step, jnp.zeros((256, LANES), F32))
        result = None
        for n in range(4):
            term = total[n * 64 : n * 64 + 64] * (MSG_SCALE * radial_two[n : n + 1, :])
            result = term if result is None else result + term
        return result

    rounded_two = spread(0).astype(BF16)
    mixing_two = nt(rounded_two, mix_two[...])
    gate_two = sigmoid(mixing_two)
    layer_wide = layer_one.astype(F32)
    features = (layer_wide + mixing_two * gate_two).astype(BF16)
    hidden = nt(features, read_hidden[...])
    slope = silu_slope(hidden, sigmoid(hidden)) * read_out_row[...] * live_col
    feature_adjoint = nn(slope.astype(BF16), read_hidden[...])
    mixing_adjoint = (feature_adjoint * silu_slope(mixing_two, gate_two)).astype(BF16)
    rounded_adjoint = nn(mixing_adjoint, mix_two[...]).astype(BF16)
    mine[1] = rounded_adjoint
    halo[CENTRE * 64 : CENTRE * 64 + 64, LANES:] = rounded_adjoint
    start_all(2, -1)

    feats[...] = jnp.transpose(features.astype(F32)).astype(BF16)
    hidden_row = nt(read_hidden[...], features)
    second = jnp.sum(hidden_row * sigmoid(hidden_row) * read_out_col[...], axis=0, keepdims=True)
    first = jnp.sum(jnp.transpose(layer_wide * read_one[...]), axis=0, keepdims=True)
    energy = (first + second) * live_row
    adjoint_wide = rounded_adjoint.astype(F32)
    for n in range(4):
        scale = MSG_SCALE * radial_two[n : n + 1, :]
        pair_lhs[n * 64 : n * 64 + 64, 0:LANES] = (scale * adjoint_wide).astype(BF16)
        pair_lhs[n * 64 : n * 64 + 64, LANES:] = (scale * layer_wide).astype(BF16)
    acc[...] = jnp.zeros((3, 64, LANES), F32)
    arrived_all(2, -1)

    layer_adjoint = feature_adjoint + read_one[...] * live_col + spread(1)
    mixing_one_adjoint = (layer_adjoint * silu_slope(mixing, gate)).astype(BF16)
    invariant_adjoint = nn(mixing_one_adjoint, mix_one[...])
    scalar_adjoint = (MSG_SCALE * invariant_adjoint[:, 0:LANES]).astype(BF16)
    norm_adjoint = (2.0 * MSG_SCALE) * invariant_adjoint[:, LANES:]
    vector_adjoint = jnp.concatenate(
        [vector_msg[k * 64 : k * 64 + 64] * norm_adjoint for k in range(3)], axis=0
    ).astype(BF16)
    kinds_adjoint = jnp.concatenate(
        [nt(scalar_adjoint, table_scalar), nt(vector_adjoint, table_vector)], axis=0
    ).astype(BF16)

    def backward_one(m, carry):
        wide_cols = pl.ds(pl.multiple_of(m * 512, 512), 512)
        cols = pl.ds(pl.multiple_of(m * LANES, LANES), LANES)
        d1[...] = nn(kinds_adjoint, hot[:, wide_cols])
        ghost = [jnp.zeros((PIECE, LANES), F32) for _ in range(3)]
        for top in range(0, 64, PIECE):
            rows = pl.ds(top, PIECE)
            sep = [pre[k, rows, cols] for k in range(3)]
            inverse = pre[3, rows, cols]
            scaled = inverse * ROOT_THREE
            along, across = None, None
            turned = [None, None, None]
            for n in range(4):
                basis, slope_n = pre[4 + n, rows, cols], pre[8 + n, rows, cols]
                lanes = slice(n * LANES, (n + 1) * LANES)
                pulls = [
                    d1[64 * (k + 1) + top : 64 * (k + 1) + top + PIECE, lanes] for k in range(3)
                ]
                projected = sep[0] * pulls[0] + sep[1] * pulls[1] + sep[2] * pulls[2]
                push = (d1[top : top + PIECE, lanes] + scaled * projected) * slope_n
                along = push if along is None else along + push
                lean = basis * projected
                across = lean if across is None else across + lean
                for k in range(3):
                    term = basis * pulls[k]
                    turned[k] = term if turned[k] is None else turned[k] + term
            radial = inverse * (along - scaled * inverse * across)
            for k in range(3):
                grad = sep[k] * radial + scaled * turned[k]
                ghost[k] = ghost[k] + grad
                acc[k, rows, :] = acc[k, rows, :] - grad
        for k in range(3):
            ghosts_out[m, k : k + 1, :] = jnp.sum(ghost[k], axis=0, keepdims=True)
        return carry

    ghosts_out[...] = jnp.zeros((CHUNKS, 8, LANES), F32)
    lax.fori_loop(0, CHUNKS, backward_one, 0)
    ghosts_in[CENTRE] = ghosts_out[CENTRE // 2]
    start_all(3, 1)

    def backward_two(m, carry):
        cols = pl.ds(pl.multiple_of(m * LANES, LANES), LANES)
        d1[:, 0:LANES] = nt(pair_lhs[...], halo[cols, :])
        for top in range(0, 64, PIECE):
            rows = pl.ds(top, PIECE)
            along = None
            for n in range(4):
                push = d1[n * 64 + top : n * 64 + top + PIECE, 0:LANES] * pre[8 + n, rows, cols]
                along = push if along is None else along + push
            along = along * pre[3, rows, cols]
            for k in range(3):
                acc[k, rows, :] = acc[k, rows, :] - along * pre[k, rows, cols]
        return carry

    lax.fori_loop(0, CHUNKS, backward_two, 0)
    sums = [jnp.sum(jnp.transpose(acc[k]), axis=0, keepdims=True) for k in range(3)]
    arrived_all(3, 1)

    even, odd = ghosts_in[0], ghosts_in[1]
    for o in range(2, OFFSETS):
        if o % 2:
            odd = odd + ghosts_in[o]
        else:
            even = even + ghosts_in[o]
    for k in range(3):
        back = even[k : k + 1, 0:64] + odd[k : k + 1, 64:LANES]
        out[k : k + 1, :] = -(sums[k] + back)
    out[3:4, :] = energy

    for phase, sign in ((0, -1), (1, -1), (2, -1), (3, 1)):
        sent_all(phase, sign)


def permutation(shape):
    nx, _, nz = shape
    run = nx // nz
    pairs = []
    for gx in range(nx):
        for gz in range(nz):
            to_x, to_z = gz * run + gx % run, gx // run
            pairs.append((gx * nz + gz, to_x * nz + to_z))
    return pairs


def local(
    shape,
    positions,
    species,
    counts,
    embed,
    radial_one,
    mix_one,
    read_one,
    radial_two,
    mix_two,
    read_hidden,
    read_out,
):
    slots = positions.shape[-1]
    occupied = (jnp.arange(slots) < counts[0, 0, 0])[None, :]
    places = jnp.where(occupied, positions[0, 0, 0], FAR)
    kinds = jnp.where(occupied, species[0, 0], -1).astype(F32)
    packet = jnp.concatenate([places, kinds, jnp.zeros((4, slots), F32)], axis=0)
    packet = jnp.concatenate([packet, packet], axis=1)

    def moved(value):
        return lax.ppermute(value, ("gx", "gz"), permutation(shape)) if COMPACT else value

    packet = moved(packet)
    vmem = pl.BlockSpec(memory_space=pltpu.VMEM)
    out, feats = pl.pallas_call(
        functools.partial(kernel, shape),
        out_shape=(
            jax.ShapeDtypeStruct((4, slots), F32),
            jax.ShapeDtypeStruct((LANES, slots), BF16),
        ),
        in_specs=[vmem] * 10,
        out_specs=(vmem, vmem),
        scratch_shapes=[
            pltpu.VMEM((OFFSETS + 1, 8, LANES), F32),
            pltpu.VMEM((CHUNKS * LANES, 2 * LANES), BF16),
            pltpu.VMEM((2, 64, LANES), BF16),
            pltpu.VMEM((CHUNKS, 8, LANES), F32),
            pltpu.VMEM((OFFSETS, 8, LANES), F32),
            pltpu.VMEM((3, 64, LANES), F32),
            pltpu.VMEM((64, LANES), F32),
            pltpu.VMEM((256, CHUNKS * 512), BF16),
            pltpu.VMEM((256, CHUNKS * LANES), BF16),
            pltpu.VMEM((32, CHUNKS * 512), BF16),
            pltpu.VMEM((12, 64, CHUNKS * LANES), F32),
            pltpu.VMEM((256, 512), F32),
            pltpu.VMEM((3, 64, LANES), F32),
            pltpu.VMEM((256, 2 * LANES), BF16),
            pltpu.SemaphoreType.DMA((4, OFFSETS)),
            pltpu.SemaphoreType.DMA((4, OFFSETS)),
        ],
        compiler_params=pltpu.CompilerParams(
            collective_id=0, has_side_effects=True, vmem_limit_bytes=40 * 1024 * 1024
        ),
        name="potential",
    )(
        packet,
        embed,
        radial_one,
        mix_one,
        read_one[None, :],
        radial_two,
        mix_two,
        read_hidden,
        read_out[:, None],
        read_out[None, :],
    )
    out, feats = moved(out), moved(feats)
    return (out[None, None, None, 0:3], out[None, None, None, 3], feats[None, None, None])


def solution(mesh):
    shape = tuple(mesh.shape[name] for name in ("gx", "gy", "gz"))
    block = ("gx", "gy", "gz")
    in_specs = (P(*block, None, None), P(*block, None), P(*block)) + (P(),) * 8
    out_specs = (P(*block, None, None), P(*block, None), P(*block, None, None))
    step = functools.partial(local, shape)
    return jax.shard_map(step, mesh=mesh, in_specs=in_specs, out_specs=out_specs, check_vma=False)
```

```python
import functools
import math

import jax
import jax.numpy as jnp
from jax import lax
from jax.experimental import pallas as pl
from jax.experimental.pallas import tpu as pltpu
from jax.sharding import PartitionSpec as P

CELL_SIDE = 5.0
CUT_SQUARE = 25.0
SOFTEN = 0.25
MSG_SCALE = 0.05
ROOT_THREE = math.sqrt(3.0)
WAVE = math.pi / CELL_SIDE
FAR = 1000.0
MESH = pl.DeviceIdType.MESH
OFFSETS = 27
CENTRE = 13
CHUNKS = 14
LANES = 128
PIECE = 16
COMPACT = True
BF16 = jnp.bfloat16
F32 = jnp.float32


def nt(a, b):
    return lax.dot_general(a, b, (((1,), (1,)), ((), ())), preferred_element_type=F32)


def nn(a, b):
    return jnp.dot(a, b, preferred_element_type=F32)


def sigmoid(v):
    return 1.0 / (1.0 + jnp.exp(-v))


def silu_slope(v, s):
    return s * (1.0 + v * (1.0 - s))


def cos_sin(y):
    q = y * y
    c = 1.0 / 479001600.0
    for term in (-1.0 / 3628800.0, 1.0 / 40320.0, -1.0 / 720.0, 1.0 / 24.0, -0.5, 1.0):
        c = c * q + term
    s = -1.0 / 39916800.0
    for term in (1.0 / 362880.0, -1.0 / 5040.0, 1.0 / 120.0, -1.0 / 6.0, 1.0):
        s = s * q + term
    return c, s * y


def corner(o):
    return o // 9 - 1, o // 3 % 3 - 1, o % 3 - 1


def kernel(
    shape,
    positions,
    species,
    counts,
    *refs,
):
    sources, refs = refs[:8], refs[8:]
    forces, energies, features_out = refs[:3]
    (
        embed,
        radial_one,
        mix_one,
        read_one,
        radial_two,
        mix_two,
        read_hidden,
        read_out,
    ) = refs[3:11]
    (
        packet,
        slots,
        halo,
        mine,
        sheet_out,
        sheet_in,
        ghosts_out,
        centre_out,
        ghosts_in,
        own,
        diag,
        vs,
        sm,
        hot,
        pre,
        d1,
        acc,
        pair_lhs,
        tally,
        send,
        recv,
        load,
    ) = refs[11:]
    nx, ny, nz = shape
    here = (lax.axis_index("gx"), lax.axis_index("gy"), lax.axis_index("gz"))

    run = nx // nz

    def near(index, size):
        return (
            jnp.where(index == 0, size - 1, index - 1),
            index,
            jnp.where(index == size - 1, 0, index + 1),
        )

    if COMPACT:
        block = (here[2] * run + lax.rem(here[0], run), here[1], here[0] // run)
    else:
        block = here
    block_near = [near(index, size) for index, size in zip(block, shape)]
    here_near = [near(index, size) for index, size in zip(here, shape)]

    def splits(three):
        return [(lax.rem(v, run), v // run) for v in three]

    def worker(triples, halves, o):
        ox, oy, oz = corner(o)
        bx, by, bz = triples[0][1 + ox], triples[1][1 + oy], triples[2][1 + oz]
        if not COMPACT:
            return bx, by, bz
        low_x, high_x = halves[1 + ox]
        return bz * run + low_x, by, high_x

    block_halves = splits(block_near[0]) if COMPACT else None
    here_halves = splits(here_near[0]) if COMPACT else None

    def holder(o):
        ox, oy, oz = corner(o)
        return block_near[0][1 + ox], block_near[1][1 + oy], block_near[2][1 + oz]

    def opposite(o):
        return OFFSETS - 1 - o

    def is_here(device):
        same = (device[0] == here[0]) & (device[1] == here[1])
        return same & (device[2] == here[2])

    to_worker = [worker(block_near, block_halves, opposite(o)) for o in range(OFFSETS)]
    packet_to = [worker(here_near, here_halves, opposite(o)) for o in range(OFFSETS)]
    holders = [holder(o) for o in range(OFFSETS)]
    neighbours = [o for o in range(OFFSETS) if o != CENTRE]
    farthest = sorted(neighbours, key=lambda o: -sum(abs(step) for step in corner(o)))
    selves = {}
    if COMPACT:
        for o in range(OFFSETS):
            if corner(o)[1] == 0 or ny < 3:
                selves[o] = is_here(holders[o])

    def elsewhere(o, action):
        if not COMPACT and o == CENTRE:
            return
        if o in selves:
            pl.when(jnp.logical_not(selves[o]))(action)
        else:
            action()

    def at_home(o, action):
        if not COMPACT and o == CENTRE:
            action()
        if o in selves:
            pl.when(selves[o])(action)

    def remote(src, dst, phase, o, device):
        return pltpu.make_async_remote_copy(
            src_ref=src,
            dst_ref=dst,
            send_sem=send.at[phase, o],
            recv_sem=recv.at[phase, o],
            device_id=device,
            device_id_type=MESH,
        )

    def coordinates(o):
        return remote(packet, slots.at[o], 0, o, packet_to[o])

    def channels(phase, o):
        dst = halo.at[phase - 1, pl.ds(o * 64, 64)]
        return remote(mine.at[phase - 1], dst, phase, o, to_worker[o])

    def ghosts(o):
        src = centre_out if o == CENTRE else ghosts_out.at[o]
        return remote(src, ghosts_in.at[o], 3, o, holders[o])

    def sheet():
        return remote(sheet_out, sheet_in, 1, CENTRE, holders[CENTRE])

    barrier = pltpu.get_barrier_semaphore()

    def greet(device):
        pl.semaphore_signal(barrier, inc=1, device_id=device, device_id_type=MESH)

    for o in range(OFFSETS):
        if COMPACT:
            elsewhere(o, functools.partial(greet, holders[o]))
    for o in neighbours:
        greet(to_worker[o])

    loads = []
    for i in range(8):
        dst = refs[3 + i]
        copy = pltpu.make_async_copy(sources[i], dst, load.at[i])
        copy.start()
        loads.append(copy)
    occupied = lax.broadcasted_iota(jnp.int32, (1, 64), 1) < counts[0, 0, 0]
    kinds = jnp.where(occupied, species[0, 0], -1).astype(F32)
    places = [jnp.where(occupied, positions[0, 0, k], FAR) for k in range(3)]
    packet[0:1, 0:64] = places[0]
    packet[0:1, 64:LANES] = places[1]
    packet[1:2, 0:64] = places[2]
    packet[1:2, 64:LANES] = kinds
    row_id = lax.broadcasted_iota(jnp.int32, (64, LANES), 0)
    lane_id = lax.broadcasted_iota(jnp.int32, (64, LANES), 1)
    diag[...] = jnp.where(row_id + 64 == lane_id, CUT_SQUARE, 0.0)
    slots[OFFSETS] = jnp.full((2, LANES), FAR, F32)
    for half in range(2):
        halo[half, OFFSETS * 64 :, :] = jnp.zeros((64, LANES), BF16)
    acc[...] = jnp.zeros((3, 64, LANES), F32)
    low = lax.broadcasted_iota(jnp.int32, (1, LANES), 1) < 64
    hot_row = lax.broadcasted_iota(jnp.int32, (32, LANES), 0).astype(F32)
    for copy in loads:
        copy.wait()
    embed_wide = embed[...].astype(F32)
    tables = []
    for g in range(2):
        rows = [radial_one[g, n : n + 1, :] * embed_wide for n in range(4)]
        tables.append(jnp.concatenate(rows, axis=0).astype(BF16))
    table_scalar, table_vector = tables

    expected = OFFSETS - 1
    if COMPACT:
        expected = expected + OFFSETS
        for flag in selves.values():
            expected = expected - jnp.where(flag, 1, 0)
    pl.semaphore_wait(barrier, expected)
    for o in farthest + [CENTRE]:
        elsewhere(o, lambda o=o: coordinates(o).start())

    def keep_packet(o):
        slots[o] = packet[...]

    for o in range(OFFSETS):
        at_home(o, functools.partial(keep_packet, o))
    for o in range(OFFSETS):
        elsewhere(o, lambda o=o: coordinates(o).wait_recv())

    own_packet = slots[CENTRE]
    column = jnp.transpose(jnp.concatenate([own_packet, jnp.zeros((6, LANES), F32)], axis=0))
    own_cols = [column[0:64, 0:1], column[64:LANES, 0:1], column[0:64, 1:2]]
    own_kind = column[64:LANES, 1:2]
    live_col = jnp.where(own_kind >= 0.0, 1.0, 0.0)
    for k in range(3):
        place = jnp.where(live_col > 0.0, own_cols[k], -FAR)
        own[k] = jnp.broadcast_to(place, (64, LANES))
    live_row = jnp.where(own_packet[1:2, 64:LANES] >= 0.0, 1.0, 0.0)
    species_id = lax.broadcasted_iota(jnp.int32, (64, 8), 1).astype(F32)
    own_hot = jnp.where(own_kind == species_id, 1.0, 0.0).astype(BF16)
    own_embed = nn(own_hot, embed[...])

    def parts(o):
        return o // 9 - 1, lax.rem(o // 3, 3) - 1, lax.rem(o, 3) - 1

    def far_rows(m):
        first, second = slots[2 * m], slots[2 * m + 1]
        first_turned, second_turned = pltpu.roll(first, 64, 1), pltpu.roll(second, 64, 1)
        shift_first, shift_second = parts(2 * m), parts(2 * m + 1)
        pairs = (
            (first[0:1], second_turned[0:1]),
            (first_turned[0:1], second[0:1]),
            (first[1:2], second_turned[1:2]),
        )
        rows = []
        for k, (a, b) in enumerate(pairs):
            a = a + shift_first[k].astype(F32) * CELL_SIDE
            b = b + shift_second[k].astype(F32) * CELL_SIDE
            rows.append(jnp.where(low, a, b))
        return rows, jnp.where(low, first_turned[1:2], second[1:2])

    def geometry(places, m, top):
        rows = pl.ds(top, PIECE)
        sep = [places[k] - own[k, rows, :] for k in range(3)]
        dist = sep[0] * sep[0] + sep[1] * sep[1] + sep[2] * sep[2] + SOFTEN
        self_pair = jnp.where(m == CENTRE // 2, 1.0, 0.0)
        dist = jnp.minimum(dist + diag[rows, :] * self_pair, CUT_SQUARE)
        inverse = lax.rsqrt(dist)
        edge = (CUT_SQUARE - dist) * (1.0 / CUT_SQUARE)
        angle = dist * inverse * WAVE - 0.5 * math.pi
        sine, minus_cosine = cos_sin(angle)
        double = -2.0 * minus_cosine
        sines = [sine, double * sine]
        sines.append(double * sines[1] - sines[0])
        sines.append(double * sines[2] - sines[1])
        return sep, inverse, edge, sines, double

    def forward(m, carry):
        places, kinds = far_rows(m)
        for n in range(4):
            hit = jnp.where(kinds == hot_row - 8.0 * n, 1.0, 0.0).astype(BF16)
            hot[:, pl.ds(pl.multiple_of(m * 512 + n * LANES, LANES), LANES)] = hit
        for top in range(0, 64, PIECE):
            sep, inverse, edge, sines, _ = geometry(places, m, top)
            weight = edge * edge * inverse
            scaled = inverse * ROOT_THREE
            units = [s * scaled for s in sep]
            for n in range(4):
                basis = sines[n] * weight
                narrow = basis.astype(BF16)
                wide_cols = pl.ds(pl.multiple_of(m * 512 + n * LANES, LANES), LANES)
                cols = pl.ds(pl.multiple_of(m * LANES, LANES), LANES)
                sm[n * 64 + top : n * 64 + top + PIECE, cols] = narrow
                vs[top : top + PIECE, wide_cols] = narrow
                for k in range(3):
                    at = 64 * (k + 1) + top
                    vs[at : at + PIECE, wide_cols] = (units[k] * basis).astype(BF16)
        return carry

    def gather_kinds(m):
        cols = pl.ds(pl.multiple_of(m * 512, 512), 512)
        tally[...] += nt(vs[:, cols], hot[:, cols])

    def forward_next(m, carry):
        gather_kinds(m - 1)
        return forward(m, carry)

    tally[...] = jnp.zeros((256, 32), F32)
    forward(jnp.int32(0), 0)
    lax.fori_loop(1, CHUNKS, forward_next, 0)
    gather_kinds(jnp.int32(CHUNKS - 1))
    kinds_sum = tally[...]
    high = kinds_sum.astype(BF16)
    rest = (kinds_sum - high.astype(F32)).astype(BF16)
    scalar_msg = MSG_SCALE * (nn(high[0:64], table_scalar) + nn(rest[0:64], table_scalar))
    vector_msg = MSG_SCALE * (nn(high[64:], table_vector) + nn(rest[64:], table_vector))
    squares = vector_msg * vector_msg
    norm = squares[0:64] + squares[64:128] + squares[128:192]
    invariants = jnp.concatenate([scalar_msg, norm], axis=1).astype(BF16)
    mixing = nt(invariants, mix_one[...])
    gate = sigmoid(mixing)
    layer_one = (own_embed + mixing * gate).astype(BF16)
    mine[0] = layer_one
    halo[0, CENTRE * 64 : CENTRE * 64 + 64, :] = layer_one
    for o in farthest:
        channels(1, o).start()

    def slopes(m, carry):
        places, _ = far_rows(m)
        cols = pl.ds(pl.multiple_of(m * LANES, LANES), LANES)
        for top in range(0, 64, PIECE):
            sep, inverse, edge, sines, double = geometry(places, m, top)
            weight = edge * edge * inverse
            fall = -edge * (4.0 / CUT_SQUARE + edge * inverse * inverse)
            cosines = [0.5 * double, 0.5 * double * double - 1.0]
            cosines.append(double * cosines[1] - cosines[0])
            cosines.append(double * cosines[2] - cosines[1])
            rows = pl.ds(top, PIECE)
            for k in range(3):
                pre[k, rows, cols] = sep[k]
            pre[3, rows, cols] = inverse
            for n in range(4):
                pre[4 + n, rows, cols] = sines[n] * weight
                turn = cosines[n] * ((n + 1) * WAVE)
                pre[8 + n, rows, cols] = turn * weight + sines[n] * fall
        return carry

    lax.fori_loop(0, CHUNKS, slopes, 0)
    for o in neighbours:
        channels(1, o).wait_recv()

    def spread(half):
        def step(j, total):
            rows = pl.ds(pl.multiple_of(j * 256, 256), 256)
            return total + nn(sm[:, rows], halo[half, rows, :])

        total = lax.fori_loop(0, 7, step, jnp.zeros((256, LANES), F32))
        result = None
        for n in range(4):
            term = total[n * 64 : n * 64 + 64] * (MSG_SCALE * radial_two[n : n + 1, :])
            result = term if result is None else result + term
        return result

    rounded_two = spread(0).astype(BF16)
    mixing_two = nt(rounded_two, mix_two[...])
    gate_two = sigmoid(mixing_two)
    layer_wide = layer_one.astype(F32)
    features = (layer_wide + mixing_two * gate_two).astype(BF16)
    hidden = nt(features, read_hidden[...])
    slope = silu_slope(hidden, sigmoid(hidden)) * read_out[...] * live_col
    feature_adjoint = nn(slope.astype(BF16), read_hidden[...])
    mixing_adjoint = (feature_adjoint * silu_slope(mixing_two, gate_two)).astype(BF16)
    rounded_adjoint = nn(mixing_adjoint, mix_two[...]).astype(BF16)
    mine[1] = rounded_adjoint
    halo[1, CENTRE * 64 : CENTRE * 64 + 64, :] = rounded_adjoint
    for o in farthest:
        channels(2, o).start()

    sheet_out[...] = features

    def keep_sheet():
        sheet_in[...] = sheet_out[...]

    second = hidden * sigmoid(hidden) * read_out[...]
    second = jnp.concatenate([second, jnp.zeros((64, LANES - 16), F32)], axis=1)
    energy = jnp.transpose(layer_wide * read_one[...] + second)
    energy = jnp.sum(energy, axis=0, keepdims=True) * live_row
    adjoint_wide = rounded_adjoint.astype(F32)
    for n in range(4):
        scale = MSG_SCALE * radial_two[n : n + 1, :]
        pair_lhs[n * 64 : n * 64 + 64, 0:LANES] = (scale * adjoint_wide).astype(BF16)
        pair_lhs[n * 64 : n * 64 + 64, LANES:] = (scale * layer_wide).astype(BF16)
    for o in neighbours:
        channels(2, o).wait_recv()
    elsewhere(CENTRE, lambda: sheet().start())
    at_home(CENTRE, keep_sheet)

    layer_adjoint = feature_adjoint + read_one[...] * live_col + spread(1)
    mixing_one_adjoint = (layer_adjoint * silu_slope(mixing, gate)).astype(BF16)
    invariant_adjoint = nn(mixing_one_adjoint, mix_one[...])
    scalar_adjoint = (MSG_SCALE * invariant_adjoint[:, 0:LANES]).astype(BF16)
    norm_adjoint = (2.0 * MSG_SCALE) * invariant_adjoint[:, LANES:]
    vector_adjoint = jnp.concatenate(
        [vector_msg[k * 64 : k * 64 + 64] * norm_adjoint for k in range(3)], axis=0
    ).astype(BF16)
    kinds_adjoint = jnp.concatenate(
        [nt(scalar_adjoint, table_scalar), nt(vector_adjoint, table_vector)], axis=0
    ).astype(BF16)

    def pulls_of(m, way):
        wide_cols = pl.ds(pl.multiple_of(m * 512, 512), 512)
        d1[way] = nn(kinds_adjoint, hot[:, wide_cols])

    def backward_one(m, way):
        cols = pl.ds(pl.multiple_of(m * LANES, LANES), LANES)
        ghost = [jnp.zeros((PIECE, LANES), F32) for _ in range(3)]
        for top in range(0, 64, PIECE):
            rows = pl.ds(top, PIECE)
            sep = [pre[k, rows, cols] for k in range(3)]
            inverse = pre[3, rows, cols]
            scaled = inverse * ROOT_THREE
            along, across = None, None
            turned = [None, None, None]
            for n in range(4):
                basis, slope_n = pre[4 + n, rows, cols], pre[8 + n, rows, cols]
                lanes = slice(n * LANES, (n + 1) * LANES)
                pulls = [
                    d1[way, 64 * (k + 1) + top : 64 * (k + 1) + top + PIECE, lanes]
                    for k in range(3)
                ]
                projected = sep[0] * pulls[0] + sep[1] * pulls[1] + sep[2] * pulls[2]
                push = (d1[way, top : top + PIECE, lanes] + scaled * projected) * slope_n
                along = push if along is None else along + push
                lean = basis * projected
                across = lean if across is None else across + lean
                for k in range(3):
                    term = basis * pulls[k]
                    turned[k] = term if turned[k] is None else turned[k] + term
            radial = inverse * (along - scaled * inverse * across)
            for k in range(3):
                grad = sep[k] * radial + scaled * turned[k]
                ghost[k] = ghost[k] + grad
                acc[k, rows, :] = acc[k, rows, :] - grad
        row = [jnp.sum(ghost[k], axis=0, keepdims=True) for k in range(3)]
        turned = [pltpu.roll(row[k], 64, 1) for k in range(3)]
        ghosts_out[2 * m, 0:1, :] = jnp.where(low, row[0], turned[1])
        ghosts_out[2 * m, 1:2, :] = jnp.where(low, row[2], 0.0)
        ghosts_out[2 * m + 1, 0:1, :] = jnp.where(low, turned[0], row[1])
        ghosts_out[2 * m + 1, 1:2, :] = jnp.where(low, turned[2], 0.0)

    pulls_of(jnp.int32(0), 0)

    def backward_pair(j, carry):
        pulls_of(2 * j + 1, 1)
        backward_one(2 * j, 0)
        pulls_of(jnp.minimum(2 * j + 2, CHUNKS - 1), 0)
        backward_one(2 * j + 1, 1)
        return carry

    lax.fori_loop(0, CHUNKS // 2, backward_pair, 0)

    def keep_ghosts(o):
        ghosts_in[o] = ghosts_out[o]

    for o in farthest:
        elsewhere(o, lambda o=o: ghosts(o).start())
    for o in neighbours:
        at_home(o, functools.partial(keep_ghosts, o))

    def backward_two(m, carry):
        cols = pl.ds(pl.multiple_of(m * LANES, LANES), LANES)
        far_channels = jnp.concatenate([halo[0, cols, :], halo[1, cols, :]], axis=1)
        d1[0, :, 0:LANES] = nt(pair_lhs[...], far_channels)
        for top in range(0, 64, PIECE):
            rows = pl.ds(top, PIECE)
            along = None
            for n in range(4):
                push = d1[0, n * 64 + top : n * 64 + top + PIECE, 0:LANES] * pre[8 + n, rows, cols]
                along = push if along is None else along + push
            along = along * pre[3, rows, cols]
            for k in range(3):
                acc[k, rows, :] = acc[k, rows, :] - along * pre[k, rows, cols]
        return carry

    lax.fori_loop(0, CHUNKS, backward_two, 0)
    sums = [jnp.sum(jnp.transpose(acc[k]), axis=0, keepdims=True) for k in range(3)]
    centre_out[0:1, :] = ghosts_out[CENTRE, 0:1, :] + jnp.concatenate(sums[0:2], axis=1)
    centre_out[1:2, :] = ghosts_out[CENTRE, 1:2, :] + jnp.concatenate([sums[2], energy], axis=1)

    def keep_centre():
        ghosts_in[CENTRE] = centre_out[...]

    elsewhere(CENTRE, lambda: ghosts(CENTRE).start())
    at_home(CENTRE, keep_centre)
    elsewhere(CENTRE, lambda: sheet().wait_recv())
    features_out[0, 0, 0] = sheet_in[...]
    for o in neighbours:
        elsewhere(o, lambda o=o: ghosts(o).wait_recv())
    total = ghosts_in[0]
    for o in neighbours[1:]:
        total = total + ghosts_in[o]
    elsewhere(CENTRE, lambda: ghosts(CENTRE).wait_recv())
    centre = ghosts_in[CENTRE]
    total = -(total + centre)
    forces[0, 0, 0] = total[0:1, 0:64]
    forces[0, 0, 1] = total[0:1, 64:LANES]
    forces[0, 0, 2] = total[1:2, 0:64]
    energies[0, 0] = centre[1:2, 64:LANES]

    for o in range(OFFSETS):
        elsewhere(o, lambda o=o: coordinates(o).wait_send())
    for o in neighbours:
        channels(1, o).wait_send()
        channels(2, o).wait_send()
    elsewhere(CENTRE, lambda: sheet().wait_send())
    for o in range(OFFSETS):
        elsewhere(o, lambda o=o: ghosts(o).wait_send())


def local(
    shape,
    positions,
    species,
    counts,
    embed,
    radial_one,
    mix_one,
    read_one,
    radial_two,
    mix_two,
    read_hidden,
    read_out,
):
    weights = (
        embed,
        radial_one,
        mix_one,
        read_one[None, :],
        radial_two,
        mix_two,
        read_hidden,
        read_out[None, :],
    )
    slots = positions.shape[-1]
    vmem = pl.BlockSpec(memory_space=pltpu.VMEM)
    positions = jnp.transpose(positions, (0, 1, 3, 2, 4))
    forces, energies, features = pl.pallas_call(
        functools.partial(kernel, shape),
        out_shape=(
            jax.ShapeDtypeStruct(positions.shape, F32),
            jax.ShapeDtypeStruct(species.shape, F32),
            jax.ShapeDtypeStruct((1, 1, 1, slots, LANES), BF16),
        ),
        in_specs=[vmem, vmem, pl.BlockSpec(memory_space=pltpu.SMEM)]
        + [pl.BlockSpec(memory_space=pl.ANY)] * 8,
        out_specs=(vmem, vmem, vmem),
        scratch_shapes=[pltpu.VMEM(w.shape, w.dtype) for w in weights]
        + [
            pltpu.VMEM((2, LANES), F32),
            pltpu.VMEM((OFFSETS + 1, 2, LANES), F32),
            pltpu.VMEM((2, CHUNKS * LANES, LANES), BF16),
            pltpu.VMEM((2, 64, LANES), BF16),
            pltpu.VMEM((64, LANES), BF16),
            pltpu.VMEM((64, LANES), BF16),
            pltpu.VMEM((OFFSETS + 1, 2, LANES), F32),
            pltpu.VMEM((2, LANES), F32),
            pltpu.VMEM((OFFSETS, 2, LANES), F32),
            pltpu.VMEM((3, 64, LANES), F32),
            pltpu.VMEM((64, LANES), F32),
            pltpu.VMEM((256, CHUNKS * 512), BF16),
            pltpu.VMEM((256, CHUNKS * LANES), BF16),
            pltpu.VMEM((32, CHUNKS * 512), BF16),
            pltpu.VMEM((12, 64, CHUNKS * LANES), F32),
            pltpu.VMEM((2, 256, 512), F32),
            pltpu.VMEM((3, 64, LANES), F32),
            pltpu.VMEM((256, 2 * LANES), BF16),
            pltpu.VMEM((256, 32), F32),
            pltpu.SemaphoreType.DMA((4, OFFSETS)),
            pltpu.SemaphoreType.DMA((4, OFFSETS)),
            pltpu.SemaphoreType.DMA((8,)),
        ],
        compiler_params=pltpu.CompilerParams(
            collective_id=0, has_side_effects=True, vmem_limit_bytes=60 * 1024 * 1024
        ),
        name="potential",
    )(positions, species, counts, *weights)
    forces = jnp.transpose(forces, (0, 1, 3, 2, 4))
    return forces, energies, jnp.swapaxes(features, 3, 4)


def solution(mesh):
    shape = tuple(mesh.shape[name] for name in ("gx", "gy", "gz"))
    block = ("gx", "gy", "gz")
    in_specs = (P(*block, None, None), P(*block, None), P(*block)) + (P(),) * 8
    out_specs = (P(*block, None, None), P(*block, None), P(*block, None, None))
    step = functools.partial(local, shape)
    return jax.shard_map(step, mesh=mesh, in_specs=in_specs, out_specs=out_specs, check_vma=False)
```

```python
import functools
import math

import jax
import jax.numpy as jnp
from jax import lax
from jax.experimental import pallas as pl
from jax.experimental.pallas import tpu as pltpu
from jax.sharding import PartitionSpec as P

CELL_SIDE = 5.0
CUT_SQUARE = 25.0
SOFTEN = 0.25
MSG_SCALE = 0.05
ROOT_THREE = math.sqrt(3.0)
WAVE = math.pi / CELL_SIDE
FAR = 1000.0
MESH = pl.DeviceIdType.MESH
OFFSETS = 27
OPERANDS = 11
CENTRE = 13
CHUNKS = 14
LANES = 128
PIECE = 16
COMPACT = True
BF16 = jnp.bfloat16
F32 = jnp.float32


def nt(a, b):
    return lax.dot_general(a, b, (((1,), (1,)), ((), ())), preferred_element_type=F32)


def nn(a, b):
    return jnp.dot(a, b, preferred_element_type=F32)


def sigmoid(v):
    return 1.0 / (1.0 + jnp.exp(-v))


def silu_slope(v, s):
    return s * (1.0 + v * (1.0 - s))


def cos_sin(y):
    q = y * y
    c = 1.0 / 479001600.0
    for term in (-1.0 / 3628800.0, 1.0 / 40320.0, -1.0 / 720.0, 1.0 / 24.0, -0.5, 1.0):
        c = c * q + term
    s = -1.0 / 39916800.0
    for term in (1.0 / 362880.0, -1.0 / 5040.0, 1.0 / 120.0, -1.0 / 6.0, 1.0):
        s = s * q + term
    return c, s * y


def corner(o):
    return o // 9 - 1, o // 3 % 3 - 1, o % 3 - 1


def meets_itself(shape, o):
    nx, ny, nz = shape
    run = nx // nz
    ox, oy, oz = corner(o)
    for gx in range(nx):
        for gz in range(nz):
            bx, bz = gz * run + gx % run, (gx // run + nz // 2) % nz
            if (bx + ox - gx) % nx == 0 and oy % ny == 0 and (bz + oz - gz) % nz == 0:
                return True
    return False


def kernel(
    shape,
    *refs,
):
    sources, refs = refs[:OPERANDS], refs[OPERANDS:]
    forces, energies, features_out = refs[:3]
    staged = refs[3 : 3 + OPERANDS]
    (
        positions,
        species,
        counts,
        embed,
        radial_one,
        mix_one,
        read_one,
        radial_two,
        mix_two,
        read_hidden,
        read_out,
    ) = staged
    (
        packet,
        slots,
        halo,
        mine,
        sheet_out,
        sheet_in,
        ghosts_out,
        centre_out,
        ghosts_in,
        own,
        diag,
        vs,
        sm,
        hot,
        pre,
        d1,
        acc,
        pair_lhs,
        tally,
        send,
        recv,
        load,
    ) = refs[3 + OPERANDS :]
    nx, ny, nz = shape
    here = (lax.axis_index("gx"), lax.axis_index("gy"), lax.axis_index("gz"))

    run = nx // nz

    def near(index, size):
        return (
            jnp.where(index == 0, size - 1, index - 1),
            index,
            jnp.where(index == size - 1, 0, index + 1),
        )

    if COMPACT:
        turned = here[0] // run + nz // 2
        block = (
            here[2] * run + lax.rem(here[0], run),
            here[1],
            jnp.where(turned >= nz, turned - nz, turned),
        )
    else:
        block = here
    block_near = [near(index, size) for index, size in zip(block, shape)]
    here_near = [near(index, size) for index, size in zip(here, shape)]

    def splits(three):
        return [(lax.rem(v, run), v // run) for v in three]

    def worker(triples, halves, o):
        ox, oy, oz = corner(o)
        bx, by, bz = triples[0][1 + ox], triples[1][1 + oy], triples[2][1 + oz]
        if not COMPACT:
            return bx, by, bz
        low_x, high_x = halves[1 + ox]
        return triples[2][4 + oz] * run + low_x, by, high_x

    def far_side(three):
        return three + tuple(
            jnp.where(v + nz // 2 >= nz, v + nz // 2 - nz, v + nz // 2) for v in three
        )

    if COMPACT:
        block_near[2] = far_side(block_near[2])
        here_near[2] = far_side(here_near[2])
    block_halves = splits(block_near[0]) if COMPACT else None
    here_halves = splits(here_near[0]) if COMPACT else None

    def holder(o):
        ox, oy, oz = corner(o)
        return block_near[0][1 + ox], block_near[1][1 + oy], block_near[2][1 + oz]

    def opposite(o):
        return OFFSETS - 1 - o

    def is_here(device):
        same = (device[0] == here[0]) & (device[1] == here[1])
        return same & (device[2] == here[2])

    to_worker = [worker(block_near, block_halves, opposite(o)) for o in range(OFFSETS)]
    packet_to = [worker(here_near, here_halves, opposite(o)) for o in range(OFFSETS)]
    holders = [holder(o) for o in range(OFFSETS)]
    neighbours = [o for o in range(OFFSETS) if o != CENTRE]
    farthest = sorted(neighbours, key=lambda o: -sum(abs(step) for step in corner(o)))
    selves = {}
    if COMPACT:
        for o in range(OFFSETS):
            if meets_itself(shape, o):
                selves[o] = is_here(holders[o])

    def elsewhere(o, action):
        if not COMPACT and o == CENTRE:
            return
        if o in selves:
            pl.when(jnp.logical_not(selves[o]))(action)
        else:
            action()

    def at_home(o, action):
        if not COMPACT and o == CENTRE:
            action()
        if o in selves:
            pl.when(selves[o])(action)

    def remote(src, dst, phase, o, device):
        return pltpu.make_async_remote_copy(
            src_ref=src,
            dst_ref=dst,
            send_sem=send.at[phase, o],
            recv_sem=recv.at[phase, o],
            device_id=device,
            device_id_type=MESH,
        )

    def coordinates(o):
        return remote(packet, slots.at[o], 0, o, packet_to[o])

    def channels(phase, o):
        dst = halo.at[phase - 1, pl.ds(o * 64, 64)]
        return remote(mine.at[phase - 1], dst, phase, o, to_worker[o])

    def ghosts(o):
        src = centre_out if o == CENTRE else ghosts_out.at[o]
        return remote(src, ghosts_in.at[o], 3, o, holders[o])

    def sheet():
        return remote(sheet_out, sheet_in, 1, CENTRE, holders[CENTRE])

    loads = []
    for i in range(OPERANDS):
        copy = pltpu.make_async_copy(sources[i], staged[i], load.at[i])
        copy.start()
        loads.append(copy)
    barrier = pltpu.get_barrier_semaphore()

    def greet(device):
        pl.semaphore_signal(barrier, inc=1, device_id=device, device_id_type=MESH)

    for o in range(OFFSETS):
        if COMPACT:
            elsewhere(o, functools.partial(greet, holders[o]))
    for o in neighbours:
        greet(to_worker[o])

    for copy in loads[:3]:
        copy.wait()
    occupied = lax.broadcasted_iota(jnp.int32, (1, 64), 1) < counts[0, 0, 0]
    kinds = jnp.where(occupied, species[0, 0], -1).astype(F32)
    places = [jnp.where(occupied, positions[0, 0, k], FAR) for k in range(3)]
    packet[0:1, 0:64] = places[0]
    packet[0:1, 64:LANES] = places[1]
    packet[1:2, 0:64] = places[2]
    packet[1:2, 64:LANES] = kinds
    row_id = lax.broadcasted_iota(jnp.int32, (64, LANES), 0)
    lane_id = lax.broadcasted_iota(jnp.int32, (64, LANES), 1)
    diag[...] = jnp.where(row_id + 64 == lane_id, CUT_SQUARE, 0.0)
    slots[OFFSETS] = jnp.full((2, LANES), FAR, F32)
    for half in range(2):
        halo[half, OFFSETS * 64 :, :] = jnp.zeros((64, LANES), BF16)
    acc[...] = jnp.zeros((3, 64, LANES), F32)
    low = lax.broadcasted_iota(jnp.int32, (1, LANES), 1) < 64
    hot_row = lax.broadcasted_iota(jnp.int32, (32, LANES), 0).astype(F32)
    for copy in loads[3:]:
        copy.wait()
    embed_wide = embed[...].astype(F32)
    tables = []
    for g in range(2):
        rows = [radial_one[g, n : n + 1, :] * embed_wide for n in range(4)]
        tables.append(jnp.concatenate(rows, axis=0).astype(BF16))
    table_scalar, table_vector = tables

    expected = OFFSETS - 1
    if COMPACT:
        expected = expected + OFFSETS
        for flag in selves.values():
            expected = expected - jnp.where(flag, 1, 0)
    pl.semaphore_wait(barrier, expected)
    for o in farthest + [CENTRE]:
        elsewhere(o, lambda o=o: coordinates(o).start())

    def keep_packet(o):
        slots[o] = packet[...]

    for o in range(OFFSETS):
        at_home(o, functools.partial(keep_packet, o))
    for o in range(OFFSETS):
        elsewhere(o, lambda o=o: coordinates(o).wait_recv())

    own_packet = slots[CENTRE]
    column = jnp.transpose(jnp.concatenate([own_packet, jnp.zeros((6, LANES), F32)], axis=0))
    own_cols = [column[0:64, 0:1], column[64:LANES, 0:1], column[0:64, 1:2]]
    own_kind = column[64:LANES, 1:2]
    live_col = jnp.where(own_kind >= 0.0, 1.0, 0.0)
    for k in range(3):
        place = jnp.where(live_col > 0.0, own_cols[k], -FAR)
        own[k] = jnp.broadcast_to(place, (64, LANES))
    live_row = jnp.where(own_packet[1:2, 64:LANES] >= 0.0, 1.0, 0.0)
    species_id = lax.broadcasted_iota(jnp.int32, (64, 8), 1).astype(F32)
    own_hot = jnp.where(own_kind == species_id, 1.0, 0.0).astype(BF16)
    own_embed = nn(own_hot, embed[...])

    def parts(o):
        return o // 9 - 1, lax.rem(o // 3, 3) - 1, lax.rem(o, 3) - 1

    def far_rows(m):
        first, second = slots[2 * m], slots[2 * m + 1]
        first_turned, second_turned = pltpu.roll(first, 64, 1), pltpu.roll(second, 64, 1)
        shift_first, shift_second = parts(2 * m), parts(2 * m + 1)
        pairs = (
            (first[0:1], second_turned[0:1]),
            (first_turned[0:1], second[0:1]),
            (first[1:2], second_turned[1:2]),
        )
        rows = []
        for k, (a, b) in enumerate(pairs):
            a = a + shift_first[k].astype(F32) * CELL_SIDE
            b = b + shift_second[k].astype(F32) * CELL_SIDE
            rows.append(jnp.where(low, a, b))
        return rows, jnp.where(low, first_turned[1:2], second[1:2])

    def geometry(places, m, top):
        rows = pl.ds(top, PIECE)
        sep = [places[k] - own[k, rows, :] for k in range(3)]
        dist = sep[0] * sep[0] + sep[1] * sep[1] + sep[2] * sep[2] + SOFTEN
        self_pair = jnp.where(m == CENTRE // 2, 1.0, 0.0)
        dist = jnp.minimum(dist + diag[rows, :] * self_pair, CUT_SQUARE)
        inverse = lax.rsqrt(dist)
        edge = (CUT_SQUARE - dist) * (1.0 / CUT_SQUARE)
        angle = dist * inverse * WAVE - 0.5 * math.pi
        sine, minus_cosine = cos_sin(angle)
        double = -2.0 * minus_cosine
        sines = [sine, double * sine]
        sines.append(double * sines[1] - sines[0])
        sines.append(double * sines[2] - sines[1])
        return sep, inverse, edge, sines, double

    def forward(m, carry):
        places, kinds = far_rows(m)
        for n in range(4):
            hit = jnp.where(kinds == hot_row - 8.0 * n, 1.0, 0.0).astype(BF16)
            hot[:, pl.ds(pl.multiple_of(m * 512 + n * LANES, LANES), LANES)] = hit
        for top in range(0, 64, PIECE):
            sep, inverse, edge, sines, _ = geometry(places, m, top)
            weight = edge * edge * inverse
            scaled = inverse * ROOT_THREE
            units = [s * scaled for s in sep]
            for n in range(4):
                basis = sines[n] * weight
                narrow = basis.astype(BF16)
                wide_cols = pl.ds(pl.multiple_of(m * 512 + n * LANES, LANES), LANES)
                cols = pl.ds(pl.multiple_of(m * LANES, LANES), LANES)
                sm[n * 64 + top : n * 64 + top + PIECE, cols] = narrow
                vs[top : top + PIECE, wide_cols] = narrow
                for k in range(3):
                    at = 64 * (k + 1) + top
                    vs[at : at + PIECE, wide_cols] = (units[k] * basis).astype(BF16)
        return carry

    def gather_kinds(m):
        cols = pl.ds(pl.multiple_of(m * 512, 512), 512)
        tally[...] += nt(vs[:, cols], hot[:, cols])

    def forward_next(m, carry):
        gather_kinds(m - 1)
        return forward(m, carry)

    tally[...] = jnp.zeros((256, 32), F32)
    forward(jnp.int32(0), 0)
    lax.fori_loop(1, CHUNKS, forward_next, 0)
    gather_kinds(jnp.int32(CHUNKS - 1))
    kinds_sum = tally[...]
    high = kinds_sum.astype(BF16)
    rest = (kinds_sum - high.astype(F32)).astype(BF16)
    scalar_msg = MSG_SCALE * (nn(high[0:64], table_scalar) + nn(rest[0:64], table_scalar))
    vector_msg = MSG_SCALE * (nn(high[64:], table_vector) + nn(rest[64:], table_vector))
    squares = vector_msg * vector_msg
    norm = squares[0:64] + squares[64:128] + squares[128:192]
    invariants = jnp.concatenate([scalar_msg, norm], axis=1).astype(BF16)
    mixing = nt(invariants, mix_one[...])
    gate = sigmoid(mixing)
    layer_one = (own_embed + mixing * gate).astype(BF16)
    mine[0] = layer_one
    halo[0, CENTRE * 64 : CENTRE * 64 + 64, :] = layer_one
    for o in farthest:
        channels(1, o).start()

    def slopes(m, carry):
        places, _ = far_rows(m)
        cols = pl.ds(pl.multiple_of(m * LANES, LANES), LANES)
        for top in range(0, 64, PIECE):
            sep, inverse, edge, sines, double = geometry(places, m, top)
            weight = edge * edge * inverse
            fall = -edge * (4.0 / CUT_SQUARE + edge * inverse * inverse)
            cosines = [0.5 * double, 0.5 * double * double - 1.0]
            cosines.append(double * cosines[1] - cosines[0])
            cosines.append(double * cosines[2] - cosines[1])
            rows = pl.ds(top, PIECE)
            for k in range(3):
                pre[k, rows, cols] = sep[k]
            pre[3, rows, cols] = inverse
            for n in range(4):
                pre[4 + n, rows, cols] = sines[n] * weight
                turn = cosines[n] * ((n + 1) * WAVE)
                pre[8 + n, rows, cols] = turn * weight + sines[n] * fall
        return carry

    lax.fori_loop(0, CHUNKS, slopes, 0)
    for o in neighbours:
        channels(1, o).wait_recv()

    def spread(half):
        def step(j, total):
            rows = pl.ds(pl.multiple_of(j * 256, 256), 256)
            return total + nn(sm[:, rows], halo[half, rows, :])

        total = lax.fori_loop(0, 7, step, jnp.zeros((256, LANES), F32))
        result = None
        for n in range(4):
            term = total[n * 64 : n * 64 + 64] * (MSG_SCALE * radial_two[n : n + 1, :])
            result = term if result is None else result + term
        return result

    rounded_two = spread(0).astype(BF16)
    mixing_two = nt(rounded_two, mix_two[...])
    gate_two = sigmoid(mixing_two)
    layer_wide = layer_one.astype(F32)
    features = (layer_wide + mixing_two * gate_two).astype(BF16)
    hidden = nt(features, read_hidden[...])
    slope = silu_slope(hidden, sigmoid(hidden)) * read_out[...] * live_col
    feature_adjoint = nn(slope.astype(BF16), read_hidden[...])
    mixing_adjoint = (feature_adjoint * silu_slope(mixing_two, gate_two)).astype(BF16)
    rounded_adjoint = nn(mixing_adjoint, mix_two[...]).astype(BF16)
    mine[1] = rounded_adjoint
    halo[1, CENTRE * 64 : CENTRE * 64 + 64, :] = rounded_adjoint
    for o in farthest:
        channels(2, o).start()

    sheet_out[...] = features

    def keep_sheet():
        sheet_in[...] = sheet_out[...]

    second = hidden * sigmoid(hidden) * read_out[...]
    second = jnp.concatenate([second, jnp.zeros((64, LANES - 16), F32)], axis=1)
    energy = jnp.transpose(layer_wide * read_one[...] + second)
    energy = jnp.sum(energy, axis=0, keepdims=True) * live_row
    adjoint_wide = rounded_adjoint.astype(F32)
    for n in range(4):
        scale = MSG_SCALE * radial_two[n : n + 1, :]
        pair_lhs[n * 64 : n * 64 + 64, 0:LANES] = (scale * adjoint_wide).astype(BF16)
        pair_lhs[n * 64 : n * 64 + 64, LANES:] = (scale * layer_wide).astype(BF16)
    for o in neighbours:
        channels(2, o).wait_recv()
    elsewhere(CENTRE, lambda: sheet().start())
    at_home(CENTRE, keep_sheet)

    layer_adjoint = feature_adjoint + read_one[...] * live_col + spread(1)
    mixing_one_adjoint = (layer_adjoint * silu_slope(mixing, gate)).astype(BF16)
    invariant_adjoint = nn(mixing_one_adjoint, mix_one[...])
    scalar_adjoint = (MSG_SCALE * invariant_adjoint[:, 0:LANES]).astype(BF16)
    norm_adjoint = (2.0 * MSG_SCALE) * invariant_adjoint[:, LANES:]
    vector_adjoint = jnp.concatenate(
        [vector_msg[k * 64 : k * 64 + 64] * norm_adjoint for k in range(3)], axis=0
    ).astype(BF16)
    kinds_adjoint = jnp.concatenate(
        [nt(scalar_adjoint, table_scalar), nt(vector_adjoint, table_vector)], axis=0
    ).astype(BF16)

    def pulls_of(m, way):
        wide_cols = pl.ds(pl.multiple_of(m * 512, 512), 512)
        d1[way] = nn(kinds_adjoint, hot[:, wide_cols])

    def backward_one(m, way):
        cols = pl.ds(pl.multiple_of(m * LANES, LANES), LANES)
        ghost = [jnp.zeros((PIECE, LANES), F32) for _ in range(3)]
        for top in range(0, 64, PIECE):
            rows = pl.ds(top, PIECE)
            sep = [pre[k, rows, cols] for k in range(3)]
            inverse = pre[3, rows, cols]
            scaled = inverse * ROOT_THREE
            along, across = None, None
            turned = [None, None, None]
            for n in range(4):
                basis, slope_n = pre[4 + n, rows, cols], pre[8 + n, rows, cols]
                lanes = slice(n * LANES, (n + 1) * LANES)
                pulls = [
                    d1[way, 64 * (k + 1) + top : 64 * (k + 1) + top + PIECE, lanes]
                    for k in range(3)
                ]
                projected = sep[0] * pulls[0] + sep[1] * pulls[1] + sep[2] * pulls[2]
                push = (d1[way, top : top + PIECE, lanes] + scaled * projected) * slope_n
                along = push if along is None else along + push
                lean = basis * projected
                across = lean if across is None else across + lean
                for k in range(3):
                    term = basis * pulls[k]
                    turned[k] = term if turned[k] is None else turned[k] + term
            radial = inverse * (along - scaled * inverse * across)
            for k in range(3):
                grad = sep[k] * radial + scaled * turned[k]
                ghost[k] = ghost[k] + grad
                acc[k, rows, :] = acc[k, rows, :] - grad
        row = [jnp.sum(ghost[k], axis=0, keepdims=True) for k in range(3)]
        turned = [pltpu.roll(row[k], 64, 1) for k in range(3)]
        ghosts_out[2 * m, 0:1, :] = jnp.where(low, row[0], turned[1])
        ghosts_out[2 * m, 1:2, :] = jnp.where(low, row[2], 0.0)
        ghosts_out[2 * m + 1, 0:1, :] = jnp.where(low, turned[0], row[1])
        ghosts_out[2 * m + 1, 1:2, :] = jnp.where(low, turned[2], 0.0)

    pulls_of(jnp.int32(0), 0)

    def backward_pair(j, carry):
        pulls_of(2 * j + 1, 1)
        backward_one(2 * j, 0)
        pulls_of(jnp.minimum(2 * j + 2, CHUNKS - 1), 0)
        backward_one(2 * j + 1, 1)
        return carry

    lax.fori_loop(0, CHUNKS // 2, backward_pair, 0)

    def keep_ghosts(o):
        ghosts_in[o] = ghosts_out[o]

    for o in farthest:
        elsewhere(o, lambda o=o: ghosts(o).start())
    for o in neighbours:
        at_home(o, functools.partial(keep_ghosts, o))

    def backward_two(m, carry):
        cols = pl.ds(pl.multiple_of(m * LANES, LANES), LANES)
        far_channels = jnp.concatenate([halo[0, cols, :], halo[1, cols, :]], axis=1)
        d1[0, :, 0:LANES] = nt(pair_lhs[...], far_channels)
        for top in range(0, 64, PIECE):
            rows = pl.ds(top, PIECE)
            along = None
            for n in range(4):
                push = d1[0, n * 64 + top : n * 64 + top + PIECE, 0:LANES] * pre[8 + n, rows, cols]
                along = push if along is None else along + push
            along = along * pre[3, rows, cols]
            for k in range(3):
                acc[k, rows, :] = acc[k, rows, :] - along * pre[k, rows, cols]
        return carry

    lax.fori_loop(0, CHUNKS, backward_two, 0)
    sums = [jnp.sum(jnp.transpose(acc[k]), axis=0, keepdims=True) for k in range(3)]
    centre_out[0:1, :] = ghosts_out[CENTRE, 0:1, :] + jnp.concatenate(sums[0:2], axis=1)
    centre_out[1:2, :] = ghosts_out[CENTRE, 1:2, :] + jnp.concatenate([sums[2], energy], axis=1)

    def keep_centre():
        ghosts_in[CENTRE] = centre_out[...]

    elsewhere(CENTRE, lambda: ghosts(CENTRE).start())
    at_home(CENTRE, keep_centre)
    elsewhere(CENTRE, lambda: sheet().wait_recv())
    features_out[0, 0, 0] = sheet_in[...]
    for o in neighbours:
        elsewhere(o, lambda o=o: ghosts(o).wait_recv())
    total = ghosts_in[0]
    for o in neighbours[1:]:
        total = total + ghosts_in[o]
    elsewhere(CENTRE, lambda: ghosts(CENTRE).wait_recv())
    centre = ghosts_in[CENTRE]
    total = -(total + centre)
    forces[0, 0, 0] = total[0:1, 0:64]
    forces[0, 0, 1] = total[0:1, 64:LANES]
    forces[0, 0, 2] = total[1:2, 0:64]
    energies[0, 0] = centre[1:2, 64:LANES]

    for o in range(OFFSETS):
        elsewhere(o, lambda o=o: coordinates(o).wait_send())
    for o in neighbours:
        channels(1, o).wait_send()
        channels(2, o).wait_send()
    elsewhere(CENTRE, lambda: sheet().wait_send())
    for o in range(OFFSETS):
        elsewhere(o, lambda o=o: ghosts(o).wait_send())


def hand_over(*refs):
    for source, target in zip(refs[:3], refs[3:]):
        target[...] = source[...]


def local(
    shape,
    positions,
    species,
    counts,
    embed,
    radial_one,
    mix_one,
    read_one,
    radial_two,
    mix_two,
    read_hidden,
    read_out,
):
    operands = (
        jnp.transpose(positions, (0, 1, 3, 2, 4)),
        species,
        counts,
        embed,
        radial_one,
        mix_one,
        read_one[None, :],
        radial_two,
        mix_two,
        read_hidden,
        read_out[None, :],
    )
    slots = positions.shape[-1]
    vmem = pl.BlockSpec(memory_space=pltpu.VMEM)
    forces, energies, features = pl.pallas_call(
        functools.partial(kernel, shape),
        out_shape=(
            jax.ShapeDtypeStruct(operands[0].shape, F32),
            jax.ShapeDtypeStruct(species.shape, F32),
            jax.ShapeDtypeStruct((1, 1, 1, slots, LANES), BF16),
        ),
        in_specs=[pl.BlockSpec(memory_space=pltpu.HBM)] * OPERANDS,
        out_specs=(vmem, vmem, vmem),
        scratch_shapes=[
            (pltpu.SMEM if w is counts else pltpu.VMEM)(w.shape, w.dtype) for w in operands
        ]
        + [
            pltpu.VMEM((2, LANES), F32),
            pltpu.VMEM((OFFSETS + 1, 2, LANES), F32),
            pltpu.VMEM((2, CHUNKS * LANES, LANES), BF16),
            pltpu.VMEM((2, 64, LANES), BF16),
            pltpu.VMEM((64, LANES), BF16),
            pltpu.VMEM((64, LANES), BF16),
            pltpu.VMEM((OFFSETS + 1, 2, LANES), F32),
            pltpu.VMEM((2, LANES), F32),
            pltpu.VMEM((OFFSETS, 2, LANES), F32),
            pltpu.VMEM((3, 64, LANES), F32),
            pltpu.VMEM((64, LANES), F32),
            pltpu.VMEM((256, CHUNKS * 512), BF16),
            pltpu.VMEM((256, CHUNKS * LANES), BF16),
            pltpu.VMEM((32, CHUNKS * 512), BF16),
            pltpu.VMEM((12, 64, CHUNKS * LANES), F32),
            pltpu.VMEM((2, 256, 512), F32),
            pltpu.VMEM((3, 64, LANES), F32),
            pltpu.VMEM((256, 2 * LANES), BF16),
            pltpu.VMEM((256, 32), F32),
            pltpu.SemaphoreType.DMA((4, OFFSETS)),
            pltpu.SemaphoreType.DMA((4, OFFSETS)),
            pltpu.SemaphoreType.DMA((OPERANDS,)),
        ],
        compiler_params=pltpu.CompilerParams(
            collective_id=0, has_side_effects=True, vmem_limit_bytes=60 * 1024 * 1024
        ),
        name="potential",
    )(*operands)
    results = (forces, energies, features)
    forces, energies, features = pl.pallas_call(
        hand_over,
        out_shape=tuple(jax.ShapeDtypeStruct(r.shape, r.dtype) for r in results),
        in_specs=[vmem] * 3,
        out_specs=(vmem, vmem, vmem),
        compiler_params=pltpu.CompilerParams(vmem_limit_bytes=60 * 1024 * 1024),
        name="hand_over",
    )(*results)
    forces = jnp.transpose(forces, (0, 1, 3, 2, 4))
    return forces, energies, jnp.swapaxes(features, 3, 4)


def solution(mesh):
    shape = tuple(mesh.shape[name] for name in ("gx", "gy", "gz"))
    block = ("gx", "gy", "gz")
    in_specs = (P(*block, None, None), P(*block, None), P(*block)) + (P(),) * 8
    out_specs = (P(*block, None, None), P(*block, None), P(*block, None, None))
    step = functools.partial(local, shape)
    return jax.shard_map(step, mesh=mesh, in_specs=in_specs, out_specs=out_specs, check_vma=False)
```

```python
import functools
import math

import jax
import jax.numpy as jnp
from jax import lax
from jax.experimental import pallas as pl
from jax.experimental.pallas import tpu as pltpu
from jax.sharding import PartitionSpec as P

CELL_SIDE = 5.0
CUT_SQUARE = 25.0
SOFTEN = 0.25
MSG_SCALE = 0.05
ROOT_THREE = math.sqrt(3.0)
WAVE = math.pi / CELL_SIDE
FAR = 1000.0
MESH = pl.DeviceIdType.MESH
OFFSETS = 27
OPERANDS = 11
CENTRE = 4
EARLY = 4
CHUNKS = 14
LANES = 128
PIECE = 16
COMPACT = True
BF16 = jnp.bfloat16
F32 = jnp.float32


def nt(a, b):
    return lax.dot_general(a, b, (((1,), (1,)), ((), ())), preferred_element_type=F32)


def nn(a, b):
    return jnp.dot(a, b, preferred_element_type=F32)


def sigmoid(v):
    return 1.0 / (1.0 + jnp.exp(-v))


def silu_slope(v, s):
    return s * (1.0 + v * (1.0 - s))


def cos_sin(y):
    q = y * y
    c = 1.0 / 479001600.0
    for term in (-1.0 / 3628800.0, 1.0 / 40320.0, -1.0 / 720.0, 1.0 / 24.0, -0.5, 1.0):
        c = c * q + term
    s = -1.0 / 39916800.0
    for term in (1.0 / 362880.0, -1.0 / 5040.0, 1.0 / 120.0, -1.0 / 6.0, 1.0):
        s = s * q + term
    return c, s * y


def corner(o):
    return o // 3 % 3 - 1, o % 3 - 1, (0, -1, 1)[o // 9]


def meets_itself(shape, o):
    nx, ny, nz = shape
    run = nx // nz
    ox, oy, oz = corner(o)
    for gx in range(nx):
        for gz in range(nz):
            bx, bz = gz * run + gx % run, (gx // run + nz // 2) % nz
            if (bx + ox - gx) % nx == 0 and oy % ny == 0 and (bz + oz - gz) % nz == 0:
                return True
    return False


def kernel(
    shape,
    *refs,
):
    sources, refs = refs[:OPERANDS], refs[OPERANDS:]
    forces, energies, features_out = refs[:3]
    staged = refs[3 : 3 + OPERANDS]
    (
        positions,
        species,
        counts,
        embed,
        radial_one,
        mix_one,
        read_one,
        radial_two,
        mix_two,
        read_hidden,
        read_out,
    ) = staged
    (
        packet,
        slots,
        halo,
        mine,
        sheet_out,
        sheet_in,
        ghosts_out,
        centre_out,
        ghosts_in,
        own,
        diag,
        vs,
        sm,
        hot,
        pre,
        d1,
        acc,
        pair_lhs,
        tally,
        send,
        recv,
        load,
    ) = refs[3 + OPERANDS :]
    nx, ny, nz = shape
    here = (lax.axis_index("gx"), lax.axis_index("gy"), lax.axis_index("gz"))

    run = nx // nz

    def near(index, size):
        return (
            jnp.where(index == 0, size - 1, index - 1),
            index,
            jnp.where(index == size - 1, 0, index + 1),
        )

    if COMPACT:
        turned = here[0] // run + nz // 2
        block = (
            here[2] * run + lax.rem(here[0], run),
            here[1],
            jnp.where(turned >= nz, turned - nz, turned),
        )
    else:
        block = here
    block_near = [near(index, size) for index, size in zip(block, shape)]
    here_near = [near(index, size) for index, size in zip(here, shape)]

    def splits(three):
        return [(lax.rem(v, run), v // run) for v in three]

    def worker(triples, halves, o):
        ox, oy, oz = corner(o)
        bx, by, bz = triples[0][1 + ox], triples[1][1 + oy], triples[2][1 + oz]
        if not COMPACT:
            return bx, by, bz
        low_x, high_x = halves[1 + ox]
        return triples[2][4 + oz] * run + low_x, by, high_x

    def far_side(three):
        return three + tuple(
            jnp.where(v + nz // 2 >= nz, v + nz // 2 - nz, v + nz // 2) for v in three
        )

    if COMPACT:
        block_near[2] = far_side(block_near[2])
        here_near[2] = far_side(here_near[2])
    block_halves = splits(block_near[0]) if COMPACT else None
    here_halves = splits(here_near[0]) if COMPACT else None

    def holder(o):
        ox, oy, oz = corner(o)
        return block_near[0][1 + ox], block_near[1][1 + oy], block_near[2][1 + oz]

    def opposite(o):
        return (0, 2, 1)[o // 9] * 9 + 8 - o % 9

    def is_here(device):
        same = (device[0] == here[0]) & (device[1] == here[1])
        return same & (device[2] == here[2])

    to_worker = [worker(block_near, block_halves, opposite(o)) for o in range(OFFSETS)]
    packet_to = [worker(here_near, here_halves, opposite(o)) for o in range(OFFSETS)]
    holders = [holder(o) for o in range(OFFSETS)]
    neighbours = [o for o in range(OFFSETS) if o != CENTRE]
    farthest = sorted(neighbours, key=lambda o: -sum(abs(step) for step in corner(o)))
    selves = {}
    if COMPACT:
        for o in range(OFFSETS):
            if meets_itself(shape, o):
                selves[o] = is_here(holders[o])

    def elsewhere(o, action):
        if not COMPACT and o == CENTRE:
            return
        if o in selves:
            pl.when(jnp.logical_not(selves[o]))(action)
        else:
            action()

    def at_home(o, action):
        if not COMPACT and o == CENTRE:
            action()
        if o in selves:
            pl.when(selves[o])(action)

    def remote(src, dst, phase, o, device):
        return pltpu.make_async_remote_copy(
            src_ref=src,
            dst_ref=dst,
            send_sem=send.at[phase, o],
            recv_sem=recv.at[phase, o],
            device_id=device,
            device_id_type=MESH,
        )

    def coordinates(o):
        return remote(packet, slots.at[o], 0, o, packet_to[o])

    def channels(phase, o):
        dst = halo.at[phase - 1, pl.ds(o * 64, 64)]
        return remote(mine.at[phase - 1], dst, phase, o, to_worker[o])

    def ghosts(o):
        src = centre_out if o == CENTRE else ghosts_out.at[o]
        return remote(src, ghosts_in.at[o], 3, o, holders[o])

    def sheet():
        return remote(sheet_out, sheet_in, 1, CENTRE, holders[CENTRE])

    loads = []
    for i in range(OPERANDS):
        copy = pltpu.make_async_copy(sources[i], staged[i], load.at[i])
        copy.start()
        loads.append(copy)
    barrier = pltpu.get_barrier_semaphore()

    def greet(device):
        pl.semaphore_signal(barrier, inc=1, device_id=device, device_id_type=MESH)

    for o in range(OFFSETS):
        if COMPACT:
            elsewhere(o, functools.partial(greet, holders[o]))
    for o in neighbours:
        greet(to_worker[o])

    for copy in loads[:3]:
        copy.wait()
    occupied = lax.broadcasted_iota(jnp.int32, (1, 64), 1) < counts[0, 0, 0]
    kinds = jnp.where(occupied, species[0, 0], -1).astype(F32)
    places = [jnp.where(occupied, positions[0, 0, k], FAR) for k in range(3)]
    packet[0:1, 0:64] = places[0]
    packet[0:1, 64:LANES] = places[1]
    packet[1:2, 0:64] = places[2]
    packet[1:2, 64:LANES] = kinds
    row_id = lax.broadcasted_iota(jnp.int32, (64, LANES), 0)
    lane_id = lax.broadcasted_iota(jnp.int32, (64, LANES), 1)
    diag[...] = jnp.where(row_id == lane_id, CUT_SQUARE, 0.0)
    slots[OFFSETS] = jnp.full((2, LANES), FAR, F32)
    for half in range(2):
        halo[half, OFFSETS * 64 :, :] = jnp.zeros((64, LANES), BF16)
    acc[...] = jnp.zeros((3, 64, LANES), F32)
    low = lax.broadcasted_iota(jnp.int32, (1, LANES), 1) < 64
    hot_row = lax.broadcasted_iota(jnp.int32, (32, LANES), 0).astype(F32)
    for copy in loads[3:]:
        copy.wait()
    embed_wide = embed[...].astype(F32)
    tables = []
    for g in range(2):
        rows = [radial_one[g, n : n + 1, :] * embed_wide for n in range(4)]
        tables.append(jnp.concatenate(rows, axis=0).astype(BF16))
    table_scalar, table_vector = tables

    expected = OFFSETS - 1
    if COMPACT:
        expected = expected + OFFSETS
        for flag in selves.values():
            expected = expected - jnp.where(flag, 1, 0)
    pl.semaphore_wait(barrier, expected)
    for o in farthest + [CENTRE]:
        elsewhere(o, lambda o=o: coordinates(o).start())

    def keep_packet(o):
        slots[o] = packet[...]

    for o in range(OFFSETS):
        at_home(o, functools.partial(keep_packet, o))
    for o in range(9):
        elsewhere(o, lambda o=o: coordinates(o).wait_recv())

    own_packet = slots[CENTRE]
    column = jnp.transpose(jnp.concatenate([own_packet, jnp.zeros((6, LANES), F32)], axis=0))
    own_cols = [column[0:64, 0:1], column[64:LANES, 0:1], column[0:64, 1:2]]
    own_kind = column[64:LANES, 1:2]
    live_col = jnp.where(own_kind >= 0.0, 1.0, 0.0)
    for k in range(3):
        place = jnp.where(live_col > 0.0, own_cols[k], -FAR)
        own[k] = jnp.broadcast_to(place, (64, LANES))
    live_row = jnp.where(own_packet[1:2, 64:LANES] >= 0.0, 1.0, 0.0)
    species_id = lax.broadcasted_iota(jnp.int32, (64, 8), 1).astype(F32)
    own_hot = jnp.where(own_kind == species_id, 1.0, 0.0).astype(BF16)
    own_embed = nn(own_hot, embed[...])

    def parts(o):
        layer = o // 9
        step = jnp.where(layer == 0, 0, jnp.where(layer == 1, -1, 1))
        return lax.rem(o // 3, 3) - 1, lax.rem(o, 3) - 1, step

    def far_rows(m):
        first, second = slots[2 * m], slots[2 * m + 1]
        first_turned, second_turned = pltpu.roll(first, 64, 1), pltpu.roll(second, 64, 1)
        shift_first, shift_second = parts(2 * m), parts(2 * m + 1)
        pairs = (
            (first[0:1], second_turned[0:1]),
            (first_turned[0:1], second[0:1]),
            (first[1:2], second_turned[1:2]),
        )
        rows = []
        for k, (a, b) in enumerate(pairs):
            a = a + shift_first[k].astype(F32) * CELL_SIDE
            b = b + shift_second[k].astype(F32) * CELL_SIDE
            rows.append(jnp.where(low, a, b))
        return rows, jnp.where(low, first_turned[1:2], second[1:2])

    def geometry(places, m, top):
        rows = pl.ds(top, PIECE)
        sep = [places[k] - own[k, rows, :] for k in range(3)]
        dist = sep[0] * sep[0] + sep[1] * sep[1] + sep[2] * sep[2] + SOFTEN
        self_pair = jnp.where(m == CENTRE // 2, 1.0, 0.0)
        dist = jnp.minimum(dist + diag[rows, :] * self_pair, CUT_SQUARE)
        inverse = lax.rsqrt(dist)
        edge = (CUT_SQUARE - dist) * (1.0 / CUT_SQUARE)
        angle = dist * inverse * WAVE - 0.5 * math.pi
        sine, minus_cosine = cos_sin(angle)
        double = -2.0 * minus_cosine
        sines = [sine, double * sine]
        sines.append(double * sines[1] - sines[0])
        sines.append(double * sines[2] - sines[1])
        return sep, inverse, edge, sines, double

    def forward(m, carry):
        places, kinds = far_rows(m)
        for n in range(4):
            hit = jnp.where(kinds == hot_row - 8.0 * n, 1.0, 0.0).astype(BF16)
            hot[:, pl.ds(pl.multiple_of(m * 512 + n * LANES, LANES), LANES)] = hit
        for top in range(0, 64, PIECE):
            sep, inverse, edge, sines, _ = geometry(places, m, top)
            weight = edge * edge * inverse
            scaled = inverse * ROOT_THREE
            units = [s * scaled for s in sep]
            for n in range(4):
                basis = sines[n] * weight
                narrow = basis.astype(BF16)
                wide_cols = pl.ds(pl.multiple_of(m * 512 + n * LANES, LANES), LANES)
                cols = pl.ds(pl.multiple_of(m * LANES, LANES), LANES)
                sm[n * 64 + top : n * 64 + top + PIECE, cols] = narrow
                vs[top : top + PIECE, wide_cols] = narrow
                for k in range(3):
                    at = 64 * (k + 1) + top
                    vs[at : at + PIECE, wide_cols] = (units[k] * basis).astype(BF16)
        return carry

    def gather_kinds(m):
        cols = pl.ds(pl.multiple_of(m * 512, 512), 512)
        tally[...] += nt(hot[:, cols], vs[:, cols])

    def forward_next(m, carry):
        gather_kinds(m - 1)
        return forward(m, carry)

    tally[...] = jnp.zeros((32, 256), F32)
    forward(jnp.int32(0), 0)
    lax.fori_loop(1, EARLY, forward_next, 0)
    for o in range(9, OFFSETS):
        elsewhere(o, lambda o=o: coordinates(o).wait_recv())
    lax.fori_loop(EARLY, CHUNKS, forward_next, 0)
    gather_kinds(jnp.int32(CHUNKS - 1))
    kinds_sum = jnp.transpose(tally[...])
    high = kinds_sum.astype(BF16)
    rest = (kinds_sum - high.astype(F32)).astype(BF16)
    scalar_msg = MSG_SCALE * (nn(high[0:64], table_scalar) + nn(rest[0:64], table_scalar))
    vector_msg = MSG_SCALE * (nn(high[64:], table_vector) + nn(rest[64:], table_vector))
    squares = vector_msg * vector_msg
    norm = squares[0:64] + squares[64:128] + squares[128:192]
    invariants = jnp.concatenate([scalar_msg, norm], axis=1).astype(BF16)
    mixing = nt(invariants, mix_one[...])
    gate = sigmoid(mixing)
    layer_one = (own_embed + mixing * gate).astype(BF16)
    mine[0] = layer_one
    halo[0, CENTRE * 64 : CENTRE * 64 + 64, :] = layer_one
    for o in farthest:
        channels(1, o).start()

    def slopes(m, carry):
        places, _ = far_rows(m)
        cols = pl.ds(pl.multiple_of(m * LANES, LANES), LANES)
        for top in range(0, 64, PIECE):
            sep, inverse, edge, sines, double = geometry(places, m, top)
            weight = edge * edge * inverse
            fall = -edge * (4.0 / CUT_SQUARE + edge * inverse * inverse)
            cosines = [0.5 * double, 0.5 * double * double - 1.0]
            cosines.append(double * cosines[1] - cosines[0])
            cosines.append(double * cosines[2] - cosines[1])
            rows = pl.ds(top, PIECE)
            for k in range(3):
                pre[k, rows, cols] = sep[k] * (inverse * ROOT_THREE)
            pre[3, rows, cols] = inverse
            for n in range(4):
                pre[4 + n, rows, cols] = sines[n] * weight
                turn = cosines[n] * ((n + 1) * WAVE)
                pre[8 + n, rows, cols] = turn * weight + sines[n] * fall
        return carry

    lax.fori_loop(0, CHUNKS, slopes, 0)
    for o in neighbours:
        channels(1, o).wait_recv()

    def spread(half):
        def step(j, total):
            rows = pl.ds(pl.multiple_of(j * 256, 256), 256)
            return total + nn(sm[:, rows], halo[half, rows, :])

        total = lax.fori_loop(0, 7, step, jnp.zeros((256, LANES), F32))
        result = None
        for n in range(4):
            term = total[n * 64 : n * 64 + 64] * (MSG_SCALE * radial_two[n : n + 1, :])
            result = term if result is None else result + term
        return result

    rounded_two = spread(0).astype(BF16)
    mixing_two = nt(rounded_two, mix_two[...])
    gate_two = sigmoid(mixing_two)
    layer_wide = layer_one.astype(F32)
    features = (layer_wide + mixing_two * gate_two).astype(BF16)
    hidden = nt(features, read_hidden[...])
    slope = silu_slope(hidden, sigmoid(hidden)) * read_out[...] * live_col
    feature_adjoint = nn(slope.astype(BF16), read_hidden[...])
    mixing_adjoint = (feature_adjoint * silu_slope(mixing_two, gate_two)).astype(BF16)
    rounded_adjoint = nn(mixing_adjoint, mix_two[...]).astype(BF16)
    mine[1] = rounded_adjoint
    halo[1, CENTRE * 64 : CENTRE * 64 + 64, :] = rounded_adjoint
    for o in farthest:
        channels(2, o).start()

    sheet_out[...] = features

    def keep_sheet():
        sheet_in[...] = sheet_out[...]

    second = hidden * sigmoid(hidden) * read_out[...]
    second = jnp.concatenate([second, jnp.zeros((64, LANES - 16), F32)], axis=1)
    energy = jnp.transpose(layer_wide * read_one[...] + second)
    energy = jnp.sum(energy, axis=0, keepdims=True) * live_row
    adjoint_wide = rounded_adjoint.astype(F32)
    for n in range(4):
        scale = MSG_SCALE * radial_two[n : n + 1, :]
        pair_lhs[n * 64 : n * 64 + 64, 0:LANES] = (scale * adjoint_wide).astype(BF16)
        pair_lhs[n * 64 : n * 64 + 64, LANES:] = (scale * layer_wide).astype(BF16)
    for o in neighbours:
        channels(2, o).wait_recv()
    elsewhere(CENTRE, lambda: sheet().start())
    at_home(CENTRE, keep_sheet)

    layer_adjoint = feature_adjoint + read_one[...] * live_col + spread(1)
    mixing_one_adjoint = (layer_adjoint * silu_slope(mixing, gate)).astype(BF16)
    invariant_adjoint = nn(mixing_one_adjoint, mix_one[...])
    scalar_adjoint = (MSG_SCALE * invariant_adjoint[:, 0:LANES]).astype(BF16)
    norm_adjoint = (2.0 * MSG_SCALE) * invariant_adjoint[:, LANES:]
    vector_adjoint = jnp.concatenate(
        [vector_msg[k * 64 : k * 64 + 64] * norm_adjoint for k in range(3)], axis=0
    ).astype(BF16)
    kinds_adjoint = jnp.concatenate(
        [nt(scalar_adjoint, table_scalar), nt(vector_adjoint, table_vector)], axis=0
    ).astype(BF16)

    def pulls_of(m, way):
        wide_cols = pl.ds(pl.multiple_of(m * 512, 512), 512)
        d1[way] = nn(kinds_adjoint, hot[:, wide_cols])

    def backward_one(m, way):
        cols = pl.ds(pl.multiple_of(m * LANES, LANES), LANES)
        ghost = [jnp.zeros((PIECE, LANES), F32) for _ in range(3)]
        for top in range(0, 64, PIECE):
            rows = pl.ds(top, PIECE)
            unit = [pre[k, rows, cols] for k in range(3)]
            inverse = pre[3, rows, cols]
            scaled = inverse * ROOT_THREE
            along, across = None, None
            turned = [None, None, None]
            for n in range(4):
                basis, slope_n = pre[4 + n, rows, cols], pre[8 + n, rows, cols]
                lanes = slice(n * LANES, (n + 1) * LANES)
                pulls = [
                    d1[way, 64 * (k + 1) + top : 64 * (k + 1) + top + PIECE, lanes]
                    for k in range(3)
                ]
                projected = unit[0] * pulls[0] + unit[1] * pulls[1] + unit[2] * pulls[2]
                push = (d1[way, top : top + PIECE, lanes] + projected) * slope_n
                along = push if along is None else along + push
                lean = basis * projected
                across = lean if across is None else across + lean
                for k in range(3):
                    term = basis * pulls[k]
                    turned[k] = term if turned[k] is None else turned[k] + term
            radial = (along - inverse * across) * (1.0 / ROOT_THREE)
            for k in range(3):
                grad = unit[k] * radial + scaled * turned[k]
                ghost[k] = ghost[k] + grad
                acc[k, rows, :] = acc[k, rows, :] - grad
        row = [jnp.sum(ghost[k], axis=0, keepdims=True) for k in range(3)]
        turned = [pltpu.roll(row[k], 64, 1) for k in range(3)]
        ghosts_out[2 * m, 0:1, :] = jnp.where(low, row[0], turned[1])
        ghosts_out[2 * m, 1:2, :] = jnp.where(low, row[2], 0.0)
        ghosts_out[2 * m + 1, 0:1, :] = jnp.where(low, turned[0], row[1])
        ghosts_out[2 * m + 1, 1:2, :] = jnp.where(low, turned[2], 0.0)

    pulls_of(jnp.int32(0), 0)

    def backward_pair(j, carry):
        pulls_of(2 * j + 1, 1)
        backward_one(2 * j, 0)
        pulls_of(jnp.minimum(2 * j + 2, CHUNKS - 1), 0)
        backward_one(2 * j + 1, 1)
        return carry


    def keep_ghosts(o):
        ghosts_in[o] = ghosts_out[o]

    def send_ghosts(first, last):
        for o in farthest:
            if first <= o < last:
                elsewhere(o, lambda o=o: ghosts(o).start())
        for o in neighbours:
            if first <= o < last:
                at_home(o, functools.partial(keep_ghosts, o))

    split = 4
    lax.fori_loop(0, split, backward_pair, 0)
    send_ghosts(0, 4 * split)
    lax.fori_loop(split, CHUNKS // 2, backward_pair, 0)
    send_ghosts(4 * split, OFFSETS)

    def backward_two(m, carry):
        cols = pl.ds(pl.multiple_of(m * LANES, LANES), LANES)
        far_channels = jnp.concatenate([halo[0, cols, :], halo[1, cols, :]], axis=1)
        d1[0, :, 0:LANES] = nt(pair_lhs[...], far_channels)
        for top in range(0, 64, PIECE):
            rows = pl.ds(top, PIECE)
            along = None
            for n in range(4):
                push = d1[0, n * 64 + top : n * 64 + top + PIECE, 0:LANES] * pre[8 + n, rows, cols]
                along = push if along is None else along + push
            along = along * (1.0 / ROOT_THREE)
            for k in range(3):
                acc[k, rows, :] = acc[k, rows, :] - along * pre[k, rows, cols]
        return carry

    lax.fori_loop(0, CHUNKS, backward_two, 0)
    sums = [jnp.sum(jnp.transpose(acc[k]), axis=0, keepdims=True) for k in range(3)]
    centre_out[0:1, :] = ghosts_out[CENTRE, 0:1, :] + jnp.concatenate(sums[0:2], axis=1)
    centre_out[1:2, :] = ghosts_out[CENTRE, 1:2, :] + jnp.concatenate([sums[2], energy], axis=1)

    def keep_centre():
        ghosts_in[CENTRE] = centre_out[...]

    elsewhere(CENTRE, lambda: ghosts(CENTRE).start())
    at_home(CENTRE, keep_centre)
    elsewhere(CENTRE, lambda: sheet().wait_recv())
    features_out[0, 0, 0] = sheet_in[...]
    for o in neighbours:
        elsewhere(o, lambda o=o: ghosts(o).wait_recv())
    total = ghosts_in[0]
    for o in neighbours[1:]:
        total = total + ghosts_in[o]
    elsewhere(CENTRE, lambda: ghosts(CENTRE).wait_recv())
    centre = ghosts_in[CENTRE]
    total = -(total + centre)
    forces[0, 0, 0] = total[0:1, 0:64]
    forces[0, 0, 1] = total[0:1, 64:LANES]
    forces[0, 0, 2] = total[1:2, 0:64]
    energies[0, 0] = centre[1:2, 64:LANES]

    for o in range(OFFSETS):
        elsewhere(o, lambda o=o: coordinates(o).wait_send())
    for o in neighbours:
        channels(1, o).wait_send()
        channels(2, o).wait_send()
    elsewhere(CENTRE, lambda: sheet().wait_send())
    for o in range(OFFSETS):
        elsewhere(o, lambda o=o: ghosts(o).wait_send())


def hand_over(*refs):
    for source, target in zip(refs[:3], refs[3:]):
        target[...] = source[...]


def local(
    shape,
    positions,
    species,
    counts,
    embed,
    radial_one,
    mix_one,
    read_one,
    radial_two,
    mix_two,
    read_hidden,
    read_out,
):
    operands = (
        jnp.transpose(positions, (0, 1, 3, 2, 4)),
        species,
        counts,
        embed,
        radial_one,
        mix_one,
        read_one[None, :],
        radial_two,
        mix_two,
        read_hidden,
        read_out[None, :],
    )
    slots = positions.shape[-1]
    vmem = pl.BlockSpec(memory_space=pltpu.VMEM)
    forces, energies, features = pl.pallas_call(
        functools.partial(kernel, shape),
        out_shape=(
            jax.ShapeDtypeStruct(operands[0].shape, F32),
            jax.ShapeDtypeStruct(species.shape, F32),
            jax.ShapeDtypeStruct((1, 1, 1, slots, LANES), BF16),
        ),
        in_specs=[pl.BlockSpec(memory_space=pltpu.HBM)] * OPERANDS,
        out_specs=(vmem, vmem, vmem),
        scratch_shapes=[
            (pltpu.SMEM if w is counts else pltpu.VMEM)(w.shape, w.dtype) for w in operands
        ]
        + [
            pltpu.VMEM((2, LANES), F32),
            pltpu.VMEM((OFFSETS + 1, 2, LANES), F32),
            pltpu.VMEM((2, CHUNKS * LANES, LANES), BF16),
            pltpu.VMEM((2, 64, LANES), BF16),
            pltpu.VMEM((64, LANES), BF16),
            pltpu.VMEM((64, LANES), BF16),
            pltpu.VMEM((OFFSETS + 1, 2, LANES), F32),
            pltpu.VMEM((2, LANES), F32),
            pltpu.VMEM((OFFSETS, 2, LANES), F32),
            pltpu.VMEM((3, 64, LANES), F32),
            pltpu.VMEM((64, LANES), F32),
            pltpu.VMEM((256, CHUNKS * 512), BF16),
            pltpu.VMEM((256, CHUNKS * LANES), BF16),
            pltpu.VMEM((32, CHUNKS * 512), BF16),
            pltpu.VMEM((12, 64, CHUNKS * LANES), F32),
            pltpu.VMEM((2, 256, 512), F32),
            pltpu.VMEM((3, 64, LANES), F32),
            pltpu.VMEM((256, 2 * LANES), BF16),
            pltpu.VMEM((32, 256), F32),
            pltpu.SemaphoreType.DMA((4, OFFSETS)),
            pltpu.SemaphoreType.DMA((4, OFFSETS)),
            pltpu.SemaphoreType.DMA((OPERANDS,)),
        ],
        compiler_params=pltpu.CompilerParams(
            collective_id=0, has_side_effects=True, vmem_limit_bytes=60 * 1024 * 1024
        ),
        name="potential",
    )(*operands)
    results = (forces, energies, features)
    forces, energies, features = pl.pallas_call(
        hand_over,
        out_shape=tuple(jax.ShapeDtypeStruct(r.shape, r.dtype) for r in results),
        in_specs=[vmem] * 3,
        out_specs=(vmem, vmem, vmem),
        compiler_params=pltpu.CompilerParams(vmem_limit_bytes=60 * 1024 * 1024),
        name="hand_over",
    )(*results)
    forces = jnp.transpose(forces, (0, 1, 3, 2, 4))
    return forces, energies, jnp.swapaxes(features, 3, 4)


def solution(mesh):
    shape = tuple(mesh.shape[name] for name in ("gx", "gy", "gz"))
    block = ("gx", "gy", "gz")
    in_specs = (P(*block, None, None), P(*block, None), P(*block)) + (P(),) * 8
    out_specs = (P(*block, None, None), P(*block, None), P(*block, None, None))
    step = functools.partial(local, shape)
    return jax.shard_map(step, mesh=mesh, in_specs=in_specs, out_specs=out_specs, check_vma=False)
```

```python
import functools
import math

import jax
import jax.numpy as jnp
from jax import lax
from jax.experimental import pallas as pl
from jax.experimental.pallas import tpu as pltpu
from jax.sharding import PartitionSpec as P

CELL_SIDE = 5.0
CUT_SQUARE = 25.0
SOFTEN = 0.25
MSG_SCALE = 0.05
ROOT_THREE = math.sqrt(3.0)
WAVE = math.pi / CELL_SIDE
FAR = 1000.0
MESH = pl.DeviceIdType.MESH
OFFSETS = 27
OPERANDS = 11
CENTRE = 4
EARLY = 4
CHUNKS = 14
LANES = 128
PIECE = 16
COMPACT = True
BF16 = jnp.bfloat16
F32 = jnp.float32


def nt(a, b):
    return lax.dot_general(a, b, (((1,), (1,)), ((), ())), preferred_element_type=F32)


def nn(a, b):
    return jnp.dot(a, b, preferred_element_type=F32)


def sigmoid(v):
    return 1.0 / (1.0 + jnp.exp(-v))


def silu_slope(v, s):
    return s * (1.0 + v * (1.0 - s))


def cos_sin(y):
    q = y * y
    c = 1.0 / 479001600.0
    for term in (-1.0 / 3628800.0, 1.0 / 40320.0, -1.0 / 720.0, 1.0 / 24.0, -0.5, 1.0):
        c = c * q + term
    s = -1.0 / 39916800.0
    for term in (1.0 / 362880.0, -1.0 / 5040.0, 1.0 / 120.0, -1.0 / 6.0, 1.0):
        s = s * q + term
    return c, s * y


def corner(o):
    return o // 3 % 3 - 1, o % 3 - 1, (0, -1, 1)[o // 9]


def meets_itself(shape, o):
    nx, ny, nz = shape
    run = nx // nz
    ox, oy, oz = corner(o)
    for gx in range(nx):
        for gz in range(nz):
            bx, bz = gz * run + gx % run, (gx // run + nz // 2) % nz
            if (bx + ox - gx) % nx == 0 and oy % ny == 0 and (bz + oz - gz) % nz == 0:
                return True
    return False


def kernel(
    shape,
    *refs,
):
    sources, refs = refs[:OPERANDS], refs[OPERANDS:]
    forces, energies, features_out = refs[:3]
    staged = refs[3 : 3 + OPERANDS]
    (
        positions,
        species,
        counts,
        embed,
        radial_one,
        mix_one,
        read_one,
        radial_two,
        mix_two,
        read_hidden,
        read_out,
    ) = staged
    (
        packet,
        slots,
        halo,
        mine,
        sheet_out,
        sheet_in,
        ghosts_out,
        centre_out,
        ghosts_in,
        own,
        diag,
        vs,
        sm,
        hot,
        pre,
        d1,
        acc,
        pair_lhs,
        tally,
        send,
        recv,
        load,
    ) = refs[3 + OPERANDS :]
    nx, ny, nz = shape
    here = (lax.axis_index("gx"), lax.axis_index("gy"), lax.axis_index("gz"))

    run = nx // nz

    def near(index, size):
        return (
            jnp.where(index == 0, size - 1, index - 1),
            index,
            jnp.where(index == size - 1, 0, index + 1),
        )

    if COMPACT:
        turned = here[0] // run + nz // 2
        block = (
            here[2] * run + lax.rem(here[0], run),
            here[1],
            jnp.where(turned >= nz, turned - nz, turned),
        )
    else:
        block = here
    block_near = [near(index, size) for index, size in zip(block, shape)]
    here_near = [near(index, size) for index, size in zip(here, shape)]

    def splits(three):
        return [(lax.rem(v, run), v // run) for v in three]

    def worker(triples, halves, o):
        ox, oy, oz = corner(o)
        bx, by, bz = triples[0][1 + ox], triples[1][1 + oy], triples[2][1 + oz]
        if not COMPACT:
            return bx, by, bz
        low_x, high_x = halves[1 + ox]
        return triples[2][4 + oz] * run + low_x, by, high_x

    def far_side(three):
        return three + tuple(
            jnp.where(v + nz // 2 >= nz, v + nz // 2 - nz, v + nz // 2) for v in three
        )

    if COMPACT:
        block_near[2] = far_side(block_near[2])
        here_near[2] = far_side(here_near[2])
    block_halves = splits(block_near[0]) if COMPACT else None
    here_halves = splits(here_near[0]) if COMPACT else None

    def holder(o):
        ox, oy, oz = corner(o)
        return block_near[0][1 + ox], block_near[1][1 + oy], block_near[2][1 + oz]

    def opposite(o):
        return (0, 2, 1)[o // 9] * 9 + 8 - o % 9

    def is_here(device):
        same = (device[0] == here[0]) & (device[1] == here[1])
        return same & (device[2] == here[2])

    to_worker = [worker(block_near, block_halves, opposite(o)) for o in range(OFFSETS)]
    packet_to = [worker(here_near, here_halves, opposite(o)) for o in range(OFFSETS)]
    holders = [holder(o) for o in range(OFFSETS)]
    neighbours = [o for o in range(OFFSETS) if o != CENTRE]
    farthest = sorted(neighbours, key=lambda o: -sum(abs(step) for step in corner(o)))
    selves = {}
    if COMPACT:
        for o in range(OFFSETS):
            if meets_itself(shape, o):
                selves[o] = is_here(holders[o])

    def elsewhere(o, action):
        if not COMPACT and o == CENTRE:
            return
        if o in selves:
            pl.when(jnp.logical_not(selves[o]))(action)
        else:
            action()

    def at_home(o, action):
        if not COMPACT and o == CENTRE:
            action()
        if o in selves:
            pl.when(selves[o])(action)

    def remote(src, dst, phase, o, device):
        return pltpu.make_async_remote_copy(
            src_ref=src,
            dst_ref=dst,
            send_sem=send.at[phase, o],
            recv_sem=recv.at[phase, o],
            device_id=device,
            device_id_type=MESH,
        )

    def coordinates(o):
        return remote(packet, slots.at[o], 0, o, packet_to[o])

    def channels(phase, o):
        dst = halo.at[phase - 1, pl.ds(o * 64, 64)]
        return remote(mine.at[phase - 1], dst, phase, o, to_worker[o])

    def ghosts(o):
        src = centre_out if o == CENTRE else ghosts_out.at[o]
        return remote(src, ghosts_in.at[o], 3, o, holders[o])

    def sheet():
        return remote(sheet_out, sheet_in, 1, CENTRE, holders[CENTRE])

    loads = []
    for i in range(OPERANDS):
        copy = pltpu.make_async_copy(sources[i], staged[i], load.at[i])
        copy.start()
        loads.append(copy)
    barrier = pltpu.get_barrier_semaphore()

    def greet(device):
        pl.semaphore_signal(barrier, inc=1, device_id=device, device_id_type=MESH)

    for o in range(OFFSETS):
        if COMPACT:
            elsewhere(o, functools.partial(greet, holders[o]))
    for o in neighbours:
        greet(to_worker[o])

    for copy in loads[:3]:
        copy.wait()
    occupied = lax.broadcasted_iota(jnp.int32, (1, 64), 1) < counts[0, 0, 0]
    kinds = jnp.where(occupied, species[0, 0], -1).astype(F32)
    places = [jnp.where(occupied, positions[0, 0, k], FAR) for k in range(3)]
    packet[0:1, 0:64] = places[0]
    packet[0:1, 64:LANES] = places[1]
    packet[1:2, 0:64] = places[2]
    packet[1:2, 64:LANES] = kinds
    row_id = lax.broadcasted_iota(jnp.int32, (64, LANES), 0)
    lane_id = lax.broadcasted_iota(jnp.int32, (64, LANES), 1)
    diag[...] = jnp.where(row_id == lane_id, CUT_SQUARE, 0.0)
    slots[OFFSETS] = jnp.full((2, LANES), FAR, F32)
    for half in range(2):
        halo[half, OFFSETS * 64 :, :] = jnp.zeros((64, LANES), BF16)
    acc[...] = jnp.zeros((3, 64, LANES), F32)
    low = lax.broadcasted_iota(jnp.int32, (1, LANES), 1) < 64
    hot_row = lax.broadcasted_iota(jnp.int32, (32, LANES), 0).astype(F32)
    for copy in loads[3:]:
        copy.wait()
    embed_wide = embed[...].astype(F32)
    tables = []
    for g in range(2):
        rows = [radial_one[g, n : n + 1, :] * embed_wide for n in range(4)]
        tables.append(jnp.concatenate(rows, axis=0).astype(BF16))
    table_scalar, table_vector = tables

    expected = OFFSETS - 1
    if COMPACT:
        expected = expected + OFFSETS
        for flag in selves.values():
            expected = expected - jnp.where(flag, 1, 0)
    pl.semaphore_wait(barrier, expected)
    for o in range(OFFSETS):
        elsewhere(o, lambda o=o: coordinates(o).start())

    def keep_packet(o):
        slots[o] = packet[...]

    for o in range(OFFSETS):
        at_home(o, functools.partial(keep_packet, o))
    for o in range(9):
        elsewhere(o, lambda o=o: coordinates(o).wait_recv())

    own_packet = slots[CENTRE]
    column = jnp.transpose(jnp.concatenate([own_packet, jnp.zeros((6, LANES), F32)], axis=0))
    own_cols = [column[0:64, 0:1], column[64:LANES, 0:1], column[0:64, 1:2]]
    own_kind = column[64:LANES, 1:2]
    live_col = jnp.where(own_kind >= 0.0, 1.0, 0.0)
    for k in range(3):
        place = jnp.where(live_col > 0.0, own_cols[k], -FAR)
        own[k] = jnp.broadcast_to(place, (64, LANES))
    live_row = jnp.where(own_packet[1:2, 64:LANES] >= 0.0, 1.0, 0.0)
    species_id = lax.broadcasted_iota(jnp.int32, (64, 8), 1).astype(F32)
    own_hot = jnp.where(own_kind == species_id, 1.0, 0.0).astype(BF16)
    own_embed = nn(own_hot, embed[...])

    def parts(o):
        layer = o // 9
        step = jnp.where(layer == 0, 0, jnp.where(layer == 1, -1, 1))
        return lax.rem(o // 3, 3) - 1, lax.rem(o, 3) - 1, step

    def far_rows(m):
        first, second = slots[2 * m], slots[2 * m + 1]
        first_turned, second_turned = pltpu.roll(first, 64, 1), pltpu.roll(second, 64, 1)
        shift_first, shift_second = parts(2 * m), parts(2 * m + 1)
        pairs = (
            (first[0:1], second_turned[0:1]),
            (first_turned[0:1], second[0:1]),
            (first[1:2], second_turned[1:2]),
        )
        rows = []
        for k, (a, b) in enumerate(pairs):
            a = a + shift_first[k].astype(F32) * CELL_SIDE
            b = b + shift_second[k].astype(F32) * CELL_SIDE
            rows.append(jnp.where(low, a, b))
        return rows, jnp.where(low, first_turned[1:2], second[1:2])

    def geometry(places, m, top):
        rows = pl.ds(top, PIECE)
        sep = [places[k] - own[k, rows, :] for k in range(3)]
        dist = sep[0] * sep[0] + sep[1] * sep[1] + sep[2] * sep[2] + SOFTEN
        self_pair = jnp.where(m == CENTRE // 2, 1.0, 0.0)
        dist = jnp.minimum(dist + diag[rows, :] * self_pair, CUT_SQUARE)
        inverse = lax.rsqrt(dist)
        edge = (CUT_SQUARE - dist) * (1.0 / CUT_SQUARE)
        angle = dist * inverse * WAVE - 0.5 * math.pi
        sine, minus_cosine = cos_sin(angle)
        double = -2.0 * minus_cosine
        sines = [sine, double * sine]
        sines.append(double * sines[1] - sines[0])
        sines.append(double * sines[2] - sines[1])
        return sep, inverse, edge, sines, double

    def forward(m, carry):
        places, kinds = far_rows(m)
        for n in range(4):
            hit = jnp.where(kinds == hot_row - 8.0 * n, 1.0, 0.0).astype(BF16)
            hot[:, pl.ds(pl.multiple_of(m * 512 + n * LANES, LANES), LANES)] = hit
        for top in range(0, 64, PIECE):
            sep, inverse, edge, sines, _ = geometry(places, m, top)
            weight = edge * edge * inverse
            scaled = inverse * ROOT_THREE
            units = [s * scaled for s in sep]
            for n in range(4):
                basis = sines[n] * weight
                narrow = basis.astype(BF16)
                wide_cols = pl.ds(pl.multiple_of(m * 512 + n * LANES, LANES), LANES)
                cols = pl.ds(pl.multiple_of(m * LANES, LANES), LANES)
                sm[n * 64 + top : n * 64 + top + PIECE, cols] = narrow
                vs[top : top + PIECE, wide_cols] = narrow
                for k in range(3):
                    at = 64 * (k + 1) + top
                    vs[at : at + PIECE, wide_cols] = (units[k] * basis).astype(BF16)
        return carry

    def gather_kinds(m):
        cols = pl.ds(pl.multiple_of(m * 512, 512), 512)
        tally[...] += nt(hot[:, cols], vs[:, cols])

    def forward_next(m, carry):
        gather_kinds(m - 1)
        return forward(m, carry)

    tally[...] = jnp.zeros((32, 256), F32)
    forward(jnp.int32(0), 0)
    lax.fori_loop(1, EARLY, forward_next, 0)
    for o in range(9, OFFSETS):
        elsewhere(o, lambda o=o: coordinates(o).wait_recv())
    lax.fori_loop(EARLY, CHUNKS, forward_next, 0)
    gather_kinds(jnp.int32(CHUNKS - 1))
    kinds_sum = jnp.transpose(tally[...])
    high = kinds_sum.astype(BF16)
    rest = (kinds_sum - high.astype(F32)).astype(BF16)
    scalar_msg = MSG_SCALE * (nn(high[0:64], table_scalar) + nn(rest[0:64], table_scalar))
    vector_msg = MSG_SCALE * (nn(high[64:], table_vector) + nn(rest[64:], table_vector))
    squares = vector_msg * vector_msg
    norm = squares[0:64] + squares[64:128] + squares[128:192]
    invariants = jnp.concatenate([scalar_msg, norm], axis=1).astype(BF16)
    mixing = nt(invariants, mix_one[...])
    gate = sigmoid(mixing)
    layer_one = (own_embed + mixing * gate).astype(BF16)
    mine[0] = layer_one
    halo[0, CENTRE * 64 : CENTRE * 64 + 64, :] = layer_one
    for o in farthest:
        channels(1, o).start()

    def slopes(m, carry):
        places, _ = far_rows(m)
        cols = pl.ds(pl.multiple_of(m * LANES, LANES), LANES)
        for top in range(0, 64, PIECE):
            sep, inverse, edge, sines, double = geometry(places, m, top)
            weight = edge * edge * inverse
            fall = -edge * (4.0 / CUT_SQUARE + edge * inverse * inverse)
            cosines = [0.5 * double, 0.5 * double * double - 1.0]
            cosines.append(double * cosines[1] - cosines[0])
            cosines.append(double * cosines[2] - cosines[1])
            rows = pl.ds(top, PIECE)
            for k in range(3):
                pre[k, rows, cols] = sep[k] * (inverse * ROOT_THREE)
            pre[3, rows, cols] = inverse
            for n in range(4):
                pre[4 + n, rows, cols] = sines[n] * weight
                turn = cosines[n] * ((n + 1) * WAVE)
                pre[8 + n, rows, cols] = turn * weight + sines[n] * fall
        return carry

    lax.fori_loop(0, CHUNKS, slopes, 0)

    def spread(half):
        def step(j, total):
            rows = pl.ds(pl.multiple_of(j * 256, 256), 256)
            return total + nn(sm[:, rows], halo[half, rows, :])

        for o in neighbours:
            if o < 9:
                channels(1 + half, o).wait_recv()
        total = lax.fori_loop(0, 2, step, jnp.zeros((256, LANES), F32))
        for o in neighbours:
            if o >= 9:
                channels(1 + half, o).wait_recv()
        total = lax.fori_loop(2, 7, step, total)
        result = None
        for n in range(4):
            term = total[n * 64 : n * 64 + 64] * (MSG_SCALE * radial_two[n : n + 1, :])
            result = term if result is None else result + term
        return result

    rounded_two = spread(0).astype(BF16)
    mixing_two = nt(rounded_two, mix_two[...])
    gate_two = sigmoid(mixing_two)
    layer_wide = layer_one.astype(F32)
    features = (layer_wide + mixing_two * gate_two).astype(BF16)
    hidden = nt(features, read_hidden[...])
    slope = silu_slope(hidden, sigmoid(hidden)) * read_out[...] * live_col
    feature_adjoint = nn(slope.astype(BF16), read_hidden[...])
    mixing_adjoint = (feature_adjoint * silu_slope(mixing_two, gate_two)).astype(BF16)
    rounded_adjoint = nn(mixing_adjoint, mix_two[...]).astype(BF16)
    mine[1] = rounded_adjoint
    halo[1, CENTRE * 64 : CENTRE * 64 + 64, :] = rounded_adjoint
    for o in farthest:
        channels(2, o).start()

    sheet_out[...] = features

    def keep_sheet():
        sheet_in[...] = sheet_out[...]

    second = hidden * sigmoid(hidden) * read_out[...]
    second = jnp.concatenate([second, jnp.zeros((64, LANES - 16), F32)], axis=1)
    energy = jnp.transpose(layer_wide * read_one[...] + second)
    energy = jnp.sum(energy, axis=0, keepdims=True) * live_row
    adjoint_wide = rounded_adjoint.astype(F32)
    for n in range(4):
        scale = MSG_SCALE * radial_two[n : n + 1, :]
        pair_lhs[n * 64 : n * 64 + 64, 0:LANES] = (scale * adjoint_wide).astype(BF16)
        pair_lhs[n * 64 : n * 64 + 64, LANES:] = (scale * layer_wide).astype(BF16)
    total_adjoint = spread(1)
    elsewhere(CENTRE, lambda: sheet().start())
    at_home(CENTRE, keep_sheet)

    layer_adjoint = feature_adjoint + read_one[...] * live_col + total_adjoint
    mixing_one_adjoint = (layer_adjoint * silu_slope(mixing, gate)).astype(BF16)
    invariant_adjoint = nn(mixing_one_adjoint, mix_one[...])
    scalar_adjoint = (MSG_SCALE * invariant_adjoint[:, 0:LANES]).astype(BF16)
    norm_adjoint = (2.0 * MSG_SCALE) * invariant_adjoint[:, LANES:]
    vector_adjoint = jnp.concatenate(
        [vector_msg[k * 64 : k * 64 + 64] * norm_adjoint for k in range(3)], axis=0
    ).astype(BF16)
    kinds_adjoint = jnp.concatenate(
        [nt(scalar_adjoint, table_scalar), nt(vector_adjoint, table_vector)], axis=0
    ).astype(BF16)

    def pulls_of(m, way):
        wide_cols = pl.ds(pl.multiple_of(m * 512, 512), 512)
        d1[way] = nn(kinds_adjoint, hot[:, wide_cols])

    def backward_one(m, way):
        cols = pl.ds(pl.multiple_of(m * LANES, LANES), LANES)
        ghost = [jnp.zeros((PIECE, LANES), F32) for _ in range(3)]
        for top in range(0, 64, PIECE):
            rows = pl.ds(top, PIECE)
            unit = [pre[k, rows, cols] for k in range(3)]
            inverse = pre[3, rows, cols]
            scaled = inverse * ROOT_THREE
            along, across = None, None
            turned = [None, None, None]
            for n in range(4):
                basis, slope_n = pre[4 + n, rows, cols], pre[8 + n, rows, cols]
                lanes = slice(n * LANES, (n + 1) * LANES)
                pulls = [
                    d1[way, 64 * (k + 1) + top : 64 * (k + 1) + top + PIECE, lanes]
                    for k in range(3)
                ]
                projected = unit[0] * pulls[0] + unit[1] * pulls[1] + unit[2] * pulls[2]
                push = (d1[way, top : top + PIECE, lanes] + projected) * slope_n
                along = push if along is None else along + push
                lean = basis * projected
                across = lean if across is None else across + lean
                for k in range(3):
                    term = basis * pulls[k]
                    turned[k] = term if turned[k] is None else turned[k] + term
            radial = (along - inverse * across) * (1.0 / ROOT_THREE)
            for k in range(3):
                grad = unit[k] * radial + scaled * turned[k]
                ghost[k] = ghost[k] + grad
                acc[k, rows, :] = acc[k, rows, :] - grad
        row = [jnp.sum(ghost[k], axis=0, keepdims=True) for k in range(3)]
        turned = [pltpu.roll(row[k], 64, 1) for k in range(3)]
        ghosts_out[2 * m, 0:1, :] = jnp.where(low, row[0], turned[1])
        ghosts_out[2 * m, 1:2, :] = jnp.where(low, row[2], 0.0)
        ghosts_out[2 * m + 1, 0:1, :] = jnp.where(low, turned[0], row[1])
        ghosts_out[2 * m + 1, 1:2, :] = jnp.where(low, turned[2], 0.0)

    pulls_of(jnp.int32(0), 0)

    def backward_pair(j, carry):
        pulls_of(2 * j + 1, 1)
        backward_one(2 * j, 0)
        pulls_of(jnp.minimum(2 * j + 2, CHUNKS - 1), 0)
        backward_one(2 * j + 1, 1)
        return carry


    def keep_ghosts(o):
        ghosts_in[o] = ghosts_out[o]

    def send_ghosts(first, last):
        for o in farthest:
            if first <= o < last:
                elsewhere(o, lambda o=o: ghosts(o).start())
        for o in neighbours:
            if first <= o < last:
                at_home(o, functools.partial(keep_ghosts, o))

    split = 4
    lax.fori_loop(0, split, backward_pair, 0)
    send_ghosts(0, 4 * split)
    lax.fori_loop(split, CHUNKS // 2, backward_pair, 0)
    send_ghosts(4 * split, OFFSETS)

    def backward_two(m, carry):
        cols = pl.ds(pl.multiple_of(m * LANES, LANES), LANES)
        far_channels = jnp.concatenate([halo[0, cols, :], halo[1, cols, :]], axis=1)
        d1[0, :, 0:LANES] = nt(pair_lhs[...], far_channels)
        for top in range(0, 64, PIECE):
            rows = pl.ds(top, PIECE)
            along = None
            for n in range(4):
                push = d1[0, n * 64 + top : n * 64 + top + PIECE, 0:LANES] * pre[8 + n, rows, cols]
                along = push if along is None else along + push
            along = along * (1.0 / ROOT_THREE)
            for k in range(3):
                acc[k, rows, :] = acc[k, rows, :] - along * pre[k, rows, cols]
        return carry

    lax.fori_loop(0, CHUNKS, backward_two, 0)
    sums = [jnp.sum(jnp.transpose(acc[k]), axis=0, keepdims=True) for k in range(3)]
    centre_out[0:1, :] = ghosts_out[CENTRE, 0:1, :] + jnp.concatenate(sums[0:2], axis=1)
    centre_out[1:2, :] = ghosts_out[CENTRE, 1:2, :] + jnp.concatenate([sums[2], energy], axis=1)

    def keep_centre():
        ghosts_in[CENTRE] = centre_out[...]

    elsewhere(CENTRE, lambda: ghosts(CENTRE).start())
    at_home(CENTRE, keep_centre)
    elsewhere(CENTRE, lambda: sheet().wait_recv())
    features_out[0, 0, 0] = sheet_in[...]
    for o in neighbours:
        elsewhere(o, lambda o=o: ghosts(o).wait_recv())
    total = ghosts_in[0]
    for o in neighbours[1:]:
        total = total + ghosts_in[o]
    elsewhere(CENTRE, lambda: ghosts(CENTRE).wait_recv())
    centre = ghosts_in[CENTRE]
    total = -(total + centre)
    forces[0, 0, 0] = total[0:1, 0:64]
    forces[0, 0, 1] = total[0:1, 64:LANES]
    forces[0, 0, 2] = total[1:2, 0:64]
    energies[0, 0] = centre[1:2, 64:LANES]

    for o in range(OFFSETS):
        elsewhere(o, lambda o=o: coordinates(o).wait_send())
    for o in neighbours:
        channels(1, o).wait_send()
        channels(2, o).wait_send()
    elsewhere(CENTRE, lambda: sheet().wait_send())
    for o in range(OFFSETS):
        elsewhere(o, lambda o=o: ghosts(o).wait_send())


def hand_over(*refs):
    for source, target in zip(refs[:3], refs[3:]):
        target[...] = source[...]


def local(
    shape,
    positions,
    species,
    counts,
    embed,
    radial_one,
    mix_one,
    read_one,
    radial_two,
    mix_two,
    read_hidden,
    read_out,
):
    operands = (
        jnp.transpose(positions, (0, 1, 3, 2, 4)),
        species,
        counts,
        embed,
        radial_one,
        mix_one,
        read_one[None, :],
        radial_two,
        mix_two,
        read_hidden,
        read_out[None, :],
    )
    slots = positions.shape[-1]
    vmem = pl.BlockSpec(memory_space=pltpu.VMEM)
    forces, energies, features = pl.pallas_call(
        functools.partial(kernel, shape),
        out_shape=(
            jax.ShapeDtypeStruct(operands[0].shape, F32),
            jax.ShapeDtypeStruct(species.shape, F32),
            jax.ShapeDtypeStruct((1, 1, 1, slots, LANES), BF16),
        ),
        in_specs=[pl.BlockSpec(memory_space=pltpu.HBM)] * OPERANDS,
        out_specs=(vmem, vmem, vmem),
        scratch_shapes=[
            (pltpu.SMEM if w is counts else pltpu.VMEM)(w.shape, w.dtype) for w in operands
        ]
        + [
            pltpu.VMEM((2, LANES), F32),
            pltpu.VMEM((OFFSETS + 1, 2, LANES), F32),
            pltpu.VMEM((2, CHUNKS * LANES, LANES), BF16),
            pltpu.VMEM((2, 64, LANES), BF16),
            pltpu.VMEM((64, LANES), BF16),
            pltpu.VMEM((64, LANES), BF16),
            pltpu.VMEM((OFFSETS + 1, 2, LANES), F32),
            pltpu.VMEM((2, LANES), F32),
            pltpu.VMEM((OFFSETS, 2, LANES), F32),
            pltpu.VMEM((3, 64, LANES), F32),
            pltpu.VMEM((64, LANES), F32),
            pltpu.VMEM((256, CHUNKS * 512), BF16),
            pltpu.VMEM((256, CHUNKS * LANES), BF16),
            pltpu.VMEM((32, CHUNKS * 512), BF16),
            pltpu.VMEM((12, 64, CHUNKS * LANES), F32),
            pltpu.VMEM((2, 256, 512), F32),
            pltpu.VMEM((3, 64, LANES), F32),
            pltpu.VMEM((256, 2 * LANES), BF16),
            pltpu.VMEM((32, 256), F32),
            pltpu.SemaphoreType.DMA((4, OFFSETS)),
            pltpu.SemaphoreType.DMA((4, OFFSETS)),
            pltpu.SemaphoreType.DMA((OPERANDS,)),
        ],
        compiler_params=pltpu.CompilerParams(
            collective_id=0, has_side_effects=True, vmem_limit_bytes=60 * 1024 * 1024
        ),
        name="potential",
    )(*operands)
    results = (forces, energies, features)
    forces, energies, features = pl.pallas_call(
        hand_over,
        out_shape=tuple(jax.ShapeDtypeStruct(r.shape, r.dtype) for r in results),
        in_specs=[vmem] * 3,
        out_specs=(vmem, vmem, vmem),
        compiler_params=pltpu.CompilerParams(vmem_limit_bytes=60 * 1024 * 1024),
        name="hand_over",
    )(*results)
    forces = jnp.transpose(forces, (0, 1, 3, 2, 4))
    return forces, energies, jnp.swapaxes(features, 3, 4)


def solution(mesh):
    shape = tuple(mesh.shape[name] for name in ("gx", "gy", "gz"))
    block = ("gx", "gy", "gz")
    in_specs = (P(*block, None, None), P(*block, None), P(*block)) + (P(),) * 8
    out_specs = (P(*block, None, None), P(*block, None), P(*block, None, None))
    step = functools.partial(local, shape)
    return jax.shard_map(step, mesh=mesh, in_specs=in_specs, out_specs=out_specs, check_vma=False)
```
